128 devices in a mesh: fsdp: 32 (over x_hi, y, z), ctx: 4 (over x_lo, core).
Axes of the slice: x: 4 (x_hi: 2, x_lo: 2; x = x_hi * 2 + x_lo), y: 4, z: 4, core: 2. Of those that a mesh axis runs over, the one named last changes fastest.
Arguments:
- token_ids: int32 [32, 512], P('fsdp', 'ctx'), may hold values from 0 to 511
- embedding: bfloat16 [512, 4096], replicated, may hold values from -15 to 15
- norm_gain: float32 [4096], replicated, may hold values from 0.5 to 1.5
- in_proj: bfloat16 [3, 4096, 4096], P(None, None, 'fsdp'), may hold values from -0.09375 to 0.09375
- short_taps: float32 [3, 3, 4096], P(None, None, 'fsdp'), may hold values from -3 to 3
- conv_taps: bfloat16 [256, 128], P('fsdp'), may hold values from -0.6 to 0.6
- out_proj: bfloat16 [4096, 4096], P('fsdp'), may hold values from -0.09375 to 0.09375
Outputs:
- output: bfloat16 [32, 512, 4096], P('fsdp', 'ctx')
The draws below stay inside these ranges and needn't reach their ends.
All inputs are finite; a program needn't handle non-finite values.
Results may differ from the reference program's by a relative error of at most 0.02.
Values may be sent and summed in bfloat16 or wider, within the bound.
A program may use at most 128 MiB of HBM per device.

```python
import math
import jax
import jax.numpy as jnp
import numpy as np
from jax import lax

D = 4096
VOCAB = 512
GROUP = 16
TAPS = 128
SHORT = 3
LEN = 512
WINDOWS = 32
GROUPS = 256
N_FSDP = 32


def draw_embedding(key, part):
    key_rows, key_cols, key_values = jax.random.split(key, 3)
    row_scale = jnp.exp(jax.random.uniform(key_rows, (VOCAB, 1), jnp.float32, math.log(0.3), math.log(3.0)))
    values = jnp.clip(jax.random.normal(key_values, (VOCAB, D), jnp.float32), -5.0, 5.0)
    col_scale = jnp.exp(jax.random.uniform(key_cols, (1, D), jnp.float32, math.log(0.5), math.log(1.0)))
    return (values * row_scale * col_scale).astype(jnp.bfloat16)


def draw_conv_taps(key, part):
    key_reach, key_rough = jax.random.split(key)
    lag_axis = jnp.arange(TAPS, dtype=jnp.float32)[None, :]
    log_reach = jax.random.uniform(key_reach, (GROUPS, 1), jnp.float32, math.log(TAPS * 0.25), math.log(TAPS * 5.0))
    rough_part = jnp.clip(jax.random.normal(key_rough, (GROUPS, TAPS), jnp.float32), -4.0, 4.0)
    return (0.15 * rough_part * jnp.exp(-lag_axis / jnp.exp(log_reach))).astype(jnp.bfloat16)


def touch_ends(array, rng, low, largest):
    longest = array.shape.index(max(array.shape))
    spots = []
    for shift in (0, 1):
        where = [jax.random.randint(jax.random.fold_in(rng, axis), (), 0, length) for axis, length in enumerate(array.shape)]
        where[longest] = (where[longest] + shift) % array.shape[longest]
        spots.append(tuple(where))
    return array.at[spots[0]].set(low).at[spots[1]].set(largest)


def block_scale(key, shape, cuts, least, high):
    loudness = 1.0
    for axis_at, blocks in cuts:
        heights = jax.random.uniform(jax.random.fold_in(jax.random.fold_in(key, 6), axis_at), (blocks,), jnp.float32, least / len(cuts), high / len(cuts))
        loudness = loudness * jnp.repeat(jnp.exp(heights), shape[axis_at] // blocks).reshape((-1,) + (1,) * (len(shape) - 1 - axis_at))
    return loudness


def rank_bounds(count, slope):
    portions = [(1 << 20) // math.isqrt(standing ** slope) + 1 for standing in range(1, count + 1)]
    scale = 1 + sum(portions) // (1 << 30)
    return np.cumsum(np.array([max(1, weight // scale) for weight in portions]))


def ranked_ids(stream_key, extent, count, lean):
    table = rank_bounds(count, lean)
    pick = jax.random.randint(jax.random.fold_in(stream_key, 1), extent, 0, int(table[count - 1]))
    rank = jnp.searchsorted(jnp.asarray(table, jnp.int32), pick, side="right")
    return jax.random.permutation(jax.random.fold_in(stream_key, 2), count)[rank].astype(jnp.int32)


def gaussian(rng, dims, spread, reach, cuts=(), kind=jnp.bfloat16):
    loudness = block_scale(rng, dims, cuts, -0.22, 0.18) if cuts else 1.0
    result = jax.random.normal(rng, dims, jnp.float32) * spread * loudness
    return jnp.minimum(jnp.maximum(result, -reach), reach).astype(kind)


def setup_inputs(seed: int = 0) -> dict:
    keys = jax.random.split(jax.random.key(seed), 8)
    token_ids = touch_ends(ranked_ids(keys[0], (WINDOWS, LEN), VOCAB, 2), jax.random.fold_in(keys[0], 3), 0, VOCAB - 1).astype(jnp.int32)
    embedding = draw_embedding(jax.random.fold_in(keys[7], 71), 0)
    norm_gain = jnp.clip(1.0 + 0.1 * jax.random.normal(keys[2], (D,), jnp.float32), 0.5, 1.5)
    in_proj = gaussian(keys[3], (3, D, D), D ** -0.5, 0.09375, ((2, 32),))
    short_taps = gaussian(keys[4], (SHORT, 3, D), 0.6, 3.0, ((2, 32),), jnp.float32)
    conv_taps = draw_conv_taps(jax.random.fold_in(keys[7], 71), 0)
    out_proj = gaussian(keys[6], (D, D), D ** -0.5, 0.09375, ((0, 32),))
    return dict(token_ids=token_ids, embedding=embedding, norm_gain=norm_gain, in_proj=in_proj, short_taps=short_taps, conv_taps=conv_taps, out_proj=out_proj)


def rms_rows(table_rows, norm_gain):
    values = table_rows.astype(jnp.float32)
    inverse_rms = lax.rsqrt(lax.optimization_barrier(jnp.mean(values * values, axis=-1, keepdims=True)) + 1e-06)
    return (values * inverse_rms * norm_gain).astype(jnp.bfloat16)

def reference(token_ids, embedding, norm_gain, in_proj, short_taps, conv_taps, out_proj):
    normed = rms_rows(embedding, norm_gain)
    proj_table = jnp.einsum('vd,ide->ive', normed.astype(jnp.float32), in_proj.astype(jnp.float32)).astype(jnp.bfloat16)
    lag_grid = (jnp.arange(LEN)[:, None] - jnp.arange(LEN)[None, :]).astype(jnp.int32)
    in_reach = (lag_grid >= 0) & (lag_grid < TAPS)
    taps_wide = conv_taps.astype(jnp.float32)
    toeplitz = jnp.where(in_reach[None], jnp.take(taps_wide, jnp.clip(lag_grid, 0, TAPS - 1), axis=1), jnp.float32(0.0))
    panel_width = D // N_FSDP
    short_reach = SHORT - 1

    def one_window(ids_row):
        projected = jnp.take(proj_table, ids_row, axis=1)
        padded = jnp.pad(projected.astype(jnp.float32), ((0, 0), (short_reach, 0), (0, 0)))
        featured = jnp.zeros(projected.shape, jnp.float32)
        for offset in range(SHORT):
            featured = featured + short_taps[offset][:, None, :] * padded[:, short_reach - offset:short_reach - offset + LEN, :]
        product = (featured[1] * featured[2]).astype(jnp.bfloat16)
        grouped = product.astype(jnp.float32).reshape(LEN, GROUPS, GROUP)
        filtered = jnp.einsum('gts,sgc->tgc', toeplitz, grouped).reshape(LEN, D)
        gated = (featured[0] * filtered).astype(jnp.bfloat16)

        def add_block(block_index, running):
            first = (block_index * panel_width).astype(jnp.int32)
            channel_cols = lax.dynamic_slice_in_dim(gated, first, panel_width, 1)
            weight_rows = lax.dynamic_slice_in_dim(out_proj, first, panel_width, 0)
            block_out = jnp.dot(channel_cols, weight_rows, preferred_element_type=jnp.float32).astype(jnp.bfloat16)
            block_out = lax.optimization_barrier(block_out)
            return running + block_out.astype(jnp.float32)
        summed = lax.fori_loop(0, N_FSDP, add_block, jnp.zeros((LEN, D), jnp.float32))
        residual = jnp.take(embedding, ids_row, axis=0).astype(jnp.float32)
        return (residual + summed).astype(jnp.bfloat16)
    return lax.map(one_window, token_ids)
```

```python
import jax
import jax.numpy as jnp
from jax import lax
from jax.experimental import pallas as pl
from jax.experimental.pallas import tpu as pltpu
from jax.sharding import PartitionSpec as P

GROUP = 16
TAPS = 128
SHORT = 3
VOCAB = 512
D = 4096
LEN = 512
CH = 32
CHUNKS = 4
CW = 512
F32 = jnp.float32
BF16 = jnp.bfloat16
MESH = pl.DeviceIdType.MESH

PA, PB, PH0, PH1, QA, QB, RA, RB = 0, 1, 2, 3, 4, 8, 12, 16
N_ROLES = 20


def dot_t(a, b):
    return lax.dot_general(a, b, (((1,), (1,)), ((), ())), preferred_element_type=F32)


def kernel(
    ids_ref, gain_ref, staps_ref, ctaps_ref, emb_ref, inp_ref, op_ref, out_ref,
    emb, inp, normed, sel, tab, ids, taps, toep, prod, qf, gsend, gath, lhs, wbuf,
    opp_s, opp_r, part, fin_s, fin_r, mine, resid, outb,
    ld_sem, wl_sem, id1_s, id1_r, id2_s, id2_r, w_s, w_r, g_s, g_r, gl_sem, b_s, b_r,
    o_s, o_r, f_s, f_r, m_s, m_r, out_sem,
):
    f = lax.axis_index("fsdp")
    c = lax.axis_index("ctx")
    xh, y, z = f // 16, (f // 4) % 4, f % 4
    xl, k = c // 2, c % 2
    x = xh * 2 + xl
    line = y * 4 + z

    def dev(xx, yy, zz, kk):
        return {"fsdp": (xx // 2) * 16 + yy * 4 + zz, "ctx": (xx % 2) * 2 + kk}

    def add(a, n):
        return (a + n) % 4

    def remote(src, dst, ssem, rsem, target):
        return pltpu.make_async_remote_copy(
            src_ref=src, dst_ref=dst, send_sem=ssem, recv_sem=rsem,
            device_id=target, device_id_type=MESH,
        )

    here = {"fsdp": f, "ctx": c}
    sent = []

    def send(src, dst, ssem, rsem, target):
        copy = remote(src, dst, ssem, rsem, target)
        copy.start()
        sent.append(copy)

    def arrived(dst, rsem):
        remote(dst, dst, rsem, rsem, here).wait_recv()

    line_peers = [(dx, dk) for dx in range(4) for dk in range(2) if (dx, dk) != (0, 0)]
    plane_peers = [(dy, dz) for dy in range(4) for dz in range(4) if (dy, dz) != (0, 0)]

    def line_dev(dx, dk):
        return dev(add(x, dx), y, z, (k + dk) % 2)

    def plane_dev(dy, dz):
        return dev(x, add(y, dy), add(z, dz), k)

    barrier = pltpu.get_barrier_semaphore()
    for dx, dk in line_peers:
        pl.semaphore_signal(barrier, inc=1, device_id=line_dev(dx, dk), device_id_type=MESH)
    for dy, dz in plane_peers:
        pl.semaphore_signal(barrier, inc=1, device_id=plane_dev(dy, dz), device_id_type=MESH)

    load_inp = pltpu.make_async_copy(inp_ref, inp, ld_sem.at[0])
    load_inp.start()
    load_emb = pltpu.make_async_copy(emb_ref, emb, ld_sem.at[1])
    load_emb.start()

    def w_source(j):
        cols = pl.multiple_of(k * (CHUNKS * CW) + j * CW, CW)
        return op_ref.at[pl.ds(pl.multiple_of(xl * 64, 64), 64), pl.ds(cols, CW)]

    own_w = []
    for j in range(CHUNKS):
        copy = pltpu.make_async_copy(w_source(j), wbuf.at[j, y, z], wl_sem.at[j])
        copy.start()
        own_w.append(copy)
    own_ids = pltpu.make_async_copy(ids_ref, ids.at[line, xh, c], ld_sem.at[2])
    own_ids.start()

    staps = jnp.concatenate(
        [staps_ref[j, :, :] for j in range(SHORT)] + [jnp.zeros((128 - 9, 128), F32)], axis=0
    )
    taps[...] = staps.T
    ch0 = pl.multiple_of(c * CH, CH)
    my_taps = taps[pl.ds(ch0, CH), :]
    tap_cols = [
        jnp.concatenate([my_taps[:, 3 * j + i : 3 * j + i + 1] for i in range(3)], axis=0)
        for j in range(SHORT)
    ]

    all_taps = ctaps_ref[...].astype(F32)
    rows8 = lax.broadcasted_iota(jnp.int32, (8, 128), 0)
    for g in range(2):
        row = jnp.sum(jnp.where(rows8 == 2 * c + g, all_taps, 0.0), axis=0, keepdims=True)
        base = jnp.concatenate([row, jnp.zeros((1, 384), F32)], axis=1)
        base = jnp.broadcast_to(base, (384, 512))
        band = pltpu.roll(base, 384, 1, stride=1, stride_axis=0)
        toep[g] = band[:, :256].astype(BF16)

    load_inp.wait()
    pick = (
        lax.broadcasted_iota(jnp.int32, (CH, 128), 1)
        == lax.broadcasted_iota(jnp.int32, (CH, 128), 0) + ch0
    )
    pick = jnp.where(pick, 1.0, 0.0).astype(BF16)
    for i in range(3):
        for d0 in range(0, D, 1024):
            sel[i * CH : (i + 1) * CH, d0 : d0 + 1024] = dot_t(
                pick, inp[i, d0 : d0 + 1024, :]
            ).astype(BF16)

    pl.semaphore_wait(barrier, len(line_peers) + len(plane_peers))

    for n, (dx, dk) in enumerate(line_peers):
        send(ids_ref, ids.at[line, xh, c], id1_s.at[n], id1_r.at[n], line_dev(dx, dk))

    def piece(j, p, q):
        return wbuf.at[j, p, q] if j % 2 == 0 else wbuf.at[j, q, p]

    def coords(j):
        return (y, z) if j % 2 == 0 else (z, y)

    def w_dev(j, dp, dq):
        return plane_dev(dp, dq) if j % 2 == 0 else plane_dev(dq, dp)

    def w_send(j, role, src, dst, dp, dq):
        send(src, dst, w_s.at[j, role], w_r.at[j, role], w_dev(j, dp, dq))

    lower, upper = pl.ds(0, 32), pl.ds(32, 32)

    def stage1(j):
        p, q = coords(j)
        src, dst = w_source(j), piece(j, p, q)
        w_send(j, PA, src, dst, 1, 0)
        w_send(j, PB, src, dst, 3, 0)
        w_send(j, QA, src, dst, 0, 1)
        w_send(j, QB, src, dst, 0, 3)

    def stage2(j):
        p, q = coords(j)
        a, b = piece(j, add(p, 3), q), piece(j, add(p, 1), q)
        arrived(a, w_r.at[j, PA])
        w_send(j, PH0, a.at[lower], a.at[lower], 1, 0)
        arrived(b, w_r.at[j, PB])
        w_send(j, PH1, b.at[upper], b.at[upper], 3, 0)
        w_send(j, QA + 1, a, a, 0, 1)
        w_send(j, QB + 1, a, a, 0, 3)
        w_send(j, QA + 2, b, b, 0, 1)
        w_send(j, QB + 2, b, b, 0, 3)

    def stage3(j):
        p, q = coords(j)
        a = piece(j, add(p, 2), q)
        arrived(a.at[lower], w_r.at[j, PH0])
        arrived(a.at[upper], w_r.at[j, PH1])
        w_send(j, QA + 3, a, a, 0, 1)
        w_send(j, QB + 3, a, a, 0, 3)

    order = (0, 3, 1, 2)

    def relay(j, i):
        p, q = coords(j)
        a = piece(j, add(p, order[i]), add(q, 3))
        b = piece(j, add(p, order[i]), add(q, 1))
        arrived(a, w_r.at[j, QA + i])
        w_send(j, RA + i, a.at[lower], a.at[lower], 0, 1)
        arrived(b, w_r.at[j, QB + i])
        w_send(j, RB + i, b.at[upper], b.at[upper], 0, 3)

    def stage4(j):
        for i in range(3):
            relay(j, i)

    def stage5(j):
        relay(j, 3)

    def stage6(j):
        p, q = coords(j)
        for i in range(4):
            a = piece(j, add(p, order[i]), add(q, 2))
            arrived(a.at[lower], w_r.at[j, RA + i])
            arrived(a.at[upper], w_r.at[j, RB + i])

    for j in range(CHUNKS):
        stage1(j)

    load_emb.wait()

    def norm_rows(b, carry):
        rows = pl.ds(pl.multiple_of(b * 32, 32), 32)
        values = emb[rows, :].astype(F32)
        inv = lax.rsqrt(jnp.mean(values * values, axis=-1, keepdims=True) + 1e-06)
        normed[rows, :] = (values * inv * gain_ref[...]).astype(BF16)
        return carry

    lax.fori_loop(0, 8, norm_rows, 0)

    own_ids.wait()
    for n, (dx, dk) in enumerate(line_peers):
        sx = add(x, 4 - dx)
        arrived(ids.at[line, sx // 2, (sx % 2) * 2 + (k + dk) % 2], id1_r.at[n])
    for n, (dy, dz) in enumerate(plane_peers):
        send(ids.at[line], ids.at[line], id2_s.at[n], id2_r.at[n], plane_dev(dy, dz))

    lax.fori_loop(8, 16, norm_rows, 0)

    table = dot_t(sel[...], normed[...]).astype(BF16)
    tab[0 : 3 * CH, :] = table[:, 0:256]
    tab[3 * CH : 6 * CH, :] = table[:, 256:512]

    own_hot = lax.broadcasted_iota(jnp.int32, (VOCAB, 128), 0) == ids_ref[...]
    own_hot = jnp.where(own_hot, 1.0, 0.0).astype(F32).T.astype(BF16)

    stage2(0)
    stage2(1)

    for n, (dy, dz) in enumerate(plane_peers):
        arrived(ids.at[add(y, 4 - dy) * 4 + add(z, 4 - dz)], id2_r.at[n])

    lane = lax.broadcasted_iota(jnp.int32, (3 * CH, LEN), 1)
    vocab = lax.broadcasted_iota(jnp.int32, (256, 128), 0)

    def mix_window(src_line, zz, h):
        hots, highs = [], []
        for b in range(4):
            row = ids[src_line, h, b]
            hots.append(jnp.where(vocab == (row & 255), 1.0, 0.0).astype(BF16))
            highs.append(row >> 8)
        hot = jnp.concatenate(hots, axis=1)
        high = jnp.concatenate(highs, axis=1)
        both = jnp.dot(tab[...], hot, preferred_element_type=F32)
        now = jnp.where(high == 1, both[3 * CH :], both[: 3 * CH])
        back1 = jnp.where(lane >= 1, pltpu.roll(now, 1, 1), 0.0)
        back2 = jnp.where(lane >= 2, pltpu.roll(now, 2, 1), 0.0)
        feat = tap_cols[0] * now + tap_cols[1] * back1 + tap_cols[2] * back2
        pr = (feat[CH : 2 * CH] * feat[2 * CH :]).astype(BF16)
        n = zz * 2 + h
        for g in range(2):
            rows = slice(g * GROUP, (g + 1) * GROUP)
            qf[g, n] = feat[rows]
            prod[g, n] = pr[rows]

    def mix_rows(yy):
        def one_line(zz, carry):
            for h in range(2):
                mix_window(yy * 4 + zz, zz, h)
            return carry

        lax.fori_loop(0, 4, one_line, 0)
        for g in range(2):
            p = prod[g].reshape(128, LEN)
            first = jnp.dot(p[:, :256], toep[g, 128:], preferred_element_type=F32)
            second = jnp.dot(p[:, 128:], toep[g], preferred_element_type=F32)
            filt = jnp.concatenate([first, second], axis=1).reshape(8, GROUP, LEN)
            for n in range(8):
                gsend[yy * 4 + n // 2, g * GROUP : (g + 1) * GROUP,
                      (n % 2) * LEN : (n % 2 + 1) * LEN] = (qf[g, n] * filt[n]).astype(BF16)

    my_rows = pl.ds(pl.multiple_of(k * CH, CH), CH)
    sib_rows = pl.ds(pl.multiple_of((1 - k) * CH, CH), CH)

    def scatter(dy):
        yy = add(y, dy)
        for dz in range(4):
            if (dy, dz) == (0, 0):
                continue
            n = dy * 4 + dz
            send(gsend.at[yy * 4 + add(z, dz)], gath.at[line, my_rows],
                 g_s.at[n], g_r.at[n], plane_dev(dy, dz))

    polls = {
        2: lambda: (stage2(2), stage2(3), stage3(0), stage3(1)),
        1: lambda: (stage4(0), stage4(1)),
        3: lambda: (stage3(2), stage3(3), stage5(0), stage5(1)),
        0: lambda: (stage4(2), stage4(3)),
    }
    for dy in (2, 1, 3, 0):
        mix_rows(add(y, dy))
        scatter(dy)
        polls[dy]()

    own_g = pltpu.make_async_copy(gsend.at[line], gath.at[line, my_rows], gl_sem)
    own_g.start()
    send(gsend.at[line], gath.at[line, my_rows], b_s.at[0], b_r.at[0], line_dev(0, 1))

    resid[...] = jnp.dot(own_hot, emb[...], preferred_element_type=F32).astype(BF16)

    for dy in (2, 1, 3, 0):
        for dz in range(4):
            if (dy, dz) == (0, 0):
                continue
            n = dy * 4 + dz
            there = gath.at[add(y, 4 - dy) * 4 + add(z, 4 - dz), my_rows]
            arrived(there, g_r.at[n])
            send(there, there, b_s.at[n], b_r.at[n], line_dev(0, 1))
    own_g.wait()
    stage5(2)
    stage5(3)
    for dy in (2, 1, 3, 0):
        sy = add(y, 4 - dy)
        for dz in range(4):
            arrived(gath.at[sy * 4 + add(z, 4 - dz), sib_rows], b_r.at[dy * 4 + dz])
        for pair in range(2):
            block = jnp.concatenate(
                [gath[sy * 4 + 2 * pair], gath[sy * 4 + 2 * pair + 1]], axis=0
            )
            cols = pl.multiple_of(sy * 256 + pair * 128, 128)
            lhs[:, pl.ds(cols, 128)] = block.T

    def block_of(dx):
        return pl.ds(pl.multiple_of(add(x, dx) * 256, 256), 256)

    def multiply(j):
        own_w[j].wait()
        stage6(j)

        def times(dx):
            w = wbuf[j].reshape(16 * 64, CW)
            return jnp.dot(lhs[block_of(dx), :], w, preferred_element_type=F32)

        far = times(2)
        opp_s[j, 0] = far[:, :256].astype(BF16)
        opp_s[j, 1] = far[:, 256:].astype(BF16)
        send(opp_s.at[j, 0], opp_r.at[j, 0], o_s.at[j, 0], o_r.at[j, 0], line_dev(1, 0))
        send(opp_s.at[j, 1], opp_r.at[j, 1], o_s.at[j, 1], o_r.at[j, 1], line_dev(3, 0))
        part[j, 0] = times(1)
        part[j, 1] = times(3)
        own = times(0).astype(BF16)
        for t in range(2):
            mine[t, j, k] = own[t * 128 : (t + 1) * 128]
        send(mine.at[1 - k, j, k], mine.at[1 - k, j, k], m_s.at[j], m_r.at[j], line_dev(0, 1))

    def pass_on(j):
        for side, dx in ((0, 1), (1, 3)):
            arrived(opp_r.at[j, side], o_r.at[j, side])
            half = slice(side * 256, (side + 1) * 256)
            rest = slice((1 - side) * 256, (2 - side) * 256)
            for t in range(2):
                rows = slice(t * 128, (t + 1) * 128)
                fin_s[j, side, t, :, half] = (
                    part[j, side, rows, half] + opp_r[j, side, rows, :].astype(F32)
                ).astype(BF16)
                fin_s[j, side, t, :, rest] = part[j, side, rows, rest].astype(BF16)
            for dk in range(2):
                t = (k + dk) % 2
                send(fin_s.at[j, side, t], fin_r.at[j, side, k],
                     f_s.at[j, side, dk], f_r.at[j, side, dk], line_dev(dx, dk))

    stores = []

    def finish(j):
        arrived(mine.at[k, j, 1 - k], m_r.at[j])
        for side in range(2):
            for dk in range(2):
                arrived(fin_r.at[j, side, (k + dk) % 2], f_r.at[j, side, dk])
        for h in range(2):
            cols = slice(h * CHUNKS * CW + j * CW, h * CHUNKS * CW + (j + 1) * CW)
            total = (
                fin_r[j, 0, h].astype(F32) + fin_r[j, 1, h].astype(F32)
                + mine[k, j, h].astype(F32) + resid[:, cols].astype(F32)
            )
            outb[:, cols] = total.astype(BF16)
            copy = pltpu.make_async_copy(
                outb.at[:, cols], out_ref.at[:, cols], out_sem.at[j, h]
            )
            copy.start()
            stores.append(copy)

    for j in range(CHUNKS):
        multiply(j)
        if j >= 1:
            pass_on(j - 1)
    pass_on(CHUNKS - 1)
    for j in range(CHUNKS):
        finish(j)

    for copy in stores:
        copy.wait()
    for copy in sent:
        copy.wait_send()


def per_device(token_ids, embedding, norm_gain, in_proj, short_taps, conv_taps, out_proj):
    vmem = pl.BlockSpec(memory_space=pltpu.VMEM)
    hbm = pl.BlockSpec(memory_space=pl.ANY)
    dma = pltpu.SemaphoreType.DMA
    out = pl.pallas_call(
        kernel,
        out_shape=jax.ShapeDtypeStruct((128, D), BF16),
        in_specs=[vmem, vmem, vmem, vmem, hbm, hbm, hbm],
        out_specs=hbm,
        scratch_shapes=[
            pltpu.VMEM((VOCAB, D), BF16),
            pltpu.VMEM((3, D, 128), BF16),
            pltpu.VMEM((VOCAB, D), BF16),
            pltpu.VMEM((3 * CH, D), BF16),
            pltpu.VMEM((6 * CH, 256), BF16),
            pltpu.VMEM((16, 2, 4, 1, 128), jnp.int32),
            pltpu.VMEM((128, 128), F32),
            pltpu.VMEM((2, 384, 256), BF16),
            pltpu.VMEM((2, 8, GROUP, LEN), BF16),
            pltpu.VMEM((2, 8, GROUP, LEN), F32),
            pltpu.VMEM((16, CH, 2 * LEN), BF16),
            pltpu.VMEM((16, 2 * CH, 2 * LEN), BF16),
            pltpu.VMEM((2 * LEN, 1024), BF16),
            pltpu.VMEM((CHUNKS, 4, 4, 64, CW), BF16),
            pltpu.VMEM((CHUNKS, 2, 256, 256), BF16),
            pltpu.VMEM((CHUNKS, 2, 256, 256), BF16),
            pltpu.VMEM((CHUNKS, 2, 256, CW), F32),
            pltpu.VMEM((CHUNKS, 2, 2, 128, CW), BF16),
            pltpu.VMEM((CHUNKS, 2, 2, 128, CW), BF16),
            pltpu.VMEM((2, CHUNKS, 2, 128, CW), BF16),
            pltpu.VMEM((128, D), BF16),
            pltpu.VMEM((128, D), BF16),
            dma((3,)), dma((CHUNKS,)), dma((7,)), dma((7,)), dma((15,)), dma((15,)),
            dma((CHUNKS, N_ROLES)), dma((CHUNKS, N_ROLES)), dma((16,)), dma((16,)), dma(()),
            dma((16,)), dma((16,)),
            dma((CHUNKS, 2)), dma((CHUNKS, 2)), dma((CHUNKS, 2, 2)), dma((CHUNKS, 2, 2)),
            dma((CHUNKS,)), dma((CHUNKS,)), dma((CHUNKS, 2)),
        ],
        compiler_params=pltpu.CompilerParams(
            collective_id=0, has_side_effects=True, vmem_limit_bytes=60 * 1024 * 1024
        ),
        name="mixer",
    )(token_ids, norm_gain.reshape(1, D), short_taps, conv_taps, embedding, in_proj, out_proj)
    return out[None]


def solution(mesh):
    return jax.shard_map(
        per_device,
        mesh=mesh,
        in_specs=(
            P("fsdp", "ctx"),
            P(),
            P(),
            P(None, None, "fsdp"),
            P(None, None, "fsdp"),
            P("fsdp", None),
            P("fsdp", None),
        ),
        out_specs=P("fsdp", "ctx", None),
        check_vma=False,
    )
```

```python
import jax
import jax.numpy as jnp
from jax import lax
from jax.experimental import pallas as pl
from jax.experimental.pallas import tpu as pltpu
from jax.sharding import PartitionSpec as P

GROUP = 16
TAPS = 128
SHORT = 3
VOCAB = 512
D = 4096
LEN = 512
CH = 32
CHUNKS = 4
CW = 512
F32 = jnp.float32
BF16 = jnp.bfloat16
MESH = pl.DeviceIdType.MESH

PA, PB, PH0, PH1, QA, QB, RA, RB = 0, 1, 2, 3, 4, 8, 12, 16
ROUND = {PA: 0, PB: 0, PH0: 1, PH1: 1, QA: 2, QA + 1: 2, QA + 2: 2, QA + 3: 3,
         QB: 2, QB + 1: 2, QB + 2: 2, QB + 3: 3, **{RA + i: 4 for i in range(8)}}
N_ONE = 13


def dot_t(a, b):
    return lax.dot_general(a, b, (((1,), (1,)), ((), ())), preferred_element_type=F32)


def kernel(
    ids_ref, gain_ref, staps_ref, ctaps_ref, emb_ref, inp_ref, op_ref, out_ref,
    emb, inp, normed, sel, tab, ids, taps, tapb, toep, prod, qf, gsend, gath, lhs, wbuf,
    opp_s, opp_r, part, fin_s, fin_r, mine, resid, outb,
    ld_sem, one_sem, w_r, g_r, b_r, o_r, f_r, m_r,
):
    wl_sem, gl_sem, out_sem, is_sem, ir_sem, i_s, i_r, w_s, g_s, b_s, o_s, f_s, m_s = (
        one_sem.at[i] for i in range(N_ONE)
    )
    f = lax.axis_index("fsdp")
    c = lax.axis_index("ctx")
    xh, y, z = f // 16, (f // 4) % 4, f % 4
    xl, k = c // 2, c % 2
    x = xh * 2 + xl
    line = y * 4 + z

    def dev(xx, yy, zz, kk):
        return {"fsdp": (xx // 2) * 16 + yy * 4 + zz, "ctx": (xx % 2) * 2 + kk}

    def add(a, n):
        return (a + n) % 4

    def remote(src, dst, ssem, rsem, target):
        return pltpu.make_async_remote_copy(
            src_ref=src, dst_ref=dst, send_sem=ssem, recv_sem=rsem,
            device_id=target, device_id_type=MESH,
        )

    here = {"fsdp": f, "ctx": c}
    def send(src, dst, ssem, rsem, target):
        remote(src, dst, ssem, rsem, target).start()

    def arrived(dst, rsem):
        remote(dst, dst, rsem, rsem, here).wait_recv()

    def all_sent(src, ssem):
        remote(src, src, ssem, ssem, here).wait_send()

    def line_dev(dx, dk):
        return dev(add(x, dx), y, z, (k + dk) % 2)

    def plane_dev(dy, dz):
        return dev(x, add(y, dy), add(z, dz), k)

    chip = line * 4 + x

    load_inp = pltpu.make_async_copy(inp_ref, inp, ld_sem.at[0])
    load_inp.start()
    load_emb = pltpu.make_async_copy(emb_ref, emb, ld_sem.at[1])
    load_emb.start()

    def w_source(j):
        cols = pl.multiple_of(k * (CHUNKS * CW) + j * CW, CW)
        return op_ref.at[pl.ds(pl.multiple_of(xl * 64, 64), 64), pl.ds(cols, CW)]

    for j in range(CHUNKS):
        pltpu.make_async_copy(w_source(j), wbuf.at[j * 16 + line], wl_sem).start()
    own_ids = pltpu.make_async_copy(ids_ref, ids.at[chip, k], ld_sem.at[2])
    own_ids.start()

    xs = [add(x, i) for i in range(4)]
    ctxs = [(xx % 2) * 2 + k for xx in xs]
    fsdps = [(xx // 2) * 16 for xx in xs]
    rows = [add(y, i) * 4 for i in range(4)]
    cols = [add(z, i) for i in range(4)]
    chips = [(dx, dy, dz) for dy in range(4) for dz in range(4) for dx in range(4)][1:]

    def chip_dev(dx, dy, dz):
        return {"fsdp": fsdps[dx] + rows[dy] + cols[dz], "ctx": ctxs[dx]}

    barrier = pltpu.get_barrier_semaphore()
    for dx in (0, 1, 3):
        pl.semaphore_signal(barrier, inc=1, device_id=line_dev(dx, 1), device_id_type=MESH)
    for d in chips:
        pl.semaphore_signal(barrier, inc=1, device_id=chip_dev(*d), device_id_type=MESH)
    staps = jnp.concatenate(
        [staps_ref[j, :, :] for j in range(SHORT)] + [jnp.zeros((128 - 9, 128), F32)], axis=0
    )
    taps[...] = staps.T
    ch0 = pl.multiple_of(c * CH, CH)
    my_taps = taps[pl.ds(ch0, CH), :]
    for j in range(SHORT):
        for i in range(3):
            tapb[j, i * CH : (i + 1) * CH, :] = jnp.broadcast_to(
                my_taps[:, 3 * j + i : 3 * j + i + 1], (CH, 128)
            )

    all_taps = ctaps_ref[...].astype(F32)
    rows8 = lax.broadcasted_iota(jnp.int32, (8, 128), 0)
    for g in range(2):
        row = jnp.sum(jnp.where(rows8 == 2 * c + g, all_taps, 0.0), axis=0, keepdims=True)
        base = jnp.concatenate([row, jnp.zeros((1, 384), F32)], axis=1)
        base = jnp.broadcast_to(base, (384, 512))
        band = pltpu.roll(base, 384, 1, stride=1, stride_axis=0)
        toep[g] = band[:, :256].astype(BF16)

    load_inp.wait()
    pick = (
        lax.broadcasted_iota(jnp.int32, (CH, 128), 1)
        == lax.broadcasted_iota(jnp.int32, (CH, 128), 0) + ch0
    )
    pick = jnp.where(pick, 1.0, 0.0).astype(BF16)
    for i in range(3):
        for d0 in range(0, D, 1024):
            sel[i * CH : (i + 1) * CH, d0 : d0 + 1024] = dot_t(
                pick, inp[i, d0 : d0 + 1024, :]
            ).astype(BF16)
    pl.semaphore_wait(barrier, 66)
    own_ids.wait()
    send(ids_ref, ids.at[chip, k], is_sem, ir_sem, line_dev(0, 1))

    def piece(j, p, q):
        return wbuf.at[j * 16 + (p * 4 + q if j % 2 == 0 else q * 4 + p)]

    def coords(j):
        return (y, z) if j % 2 == 0 else (z, y)

    def w_dev(j, dp, dq):
        return plane_dev(dp, dq) if j % 2 == 0 else plane_dev(dq, dp)

    def w_send(j, role, src, dst, dp, dq):
        send(src, dst, w_s, w_r.at[j, ROUND[role]], w_dev(j, dp, dq))

    def w_arrived(j, n, pieces):
        arrived(wbuf.at[pl.ds(j * 16, pieces)], w_r.at[j, n])

    lower, upper = pl.ds(0, 32), pl.ds(32, 32)

    def stage1(j):
        p, q = coords(j)
        src, dst = w_source(j), piece(j, p, q)
        w_send(j, PA, src, dst, 1, 0)
        w_send(j, PB, src, dst, 3, 0)
        w_send(j, QA, src, dst, 0, 1)
        w_send(j, QB, src, dst, 0, 3)

    def stage2(j):
        p, q = coords(j)
        a, b = piece(j, add(p, 3), q), piece(j, add(p, 1), q)
        w_arrived(j, 0, 2)
        w_send(j, PH0, a.at[lower], a.at[lower], 1, 0)
        w_send(j, PH1, b.at[upper], b.at[upper], 3, 0)
        w_send(j, QA + 1, a, a, 0, 1)
        w_send(j, QB + 1, a, a, 0, 3)
        w_send(j, QA + 2, b, b, 0, 1)
        w_send(j, QB + 2, b, b, 0, 3)

    def stage3(j):
        p, q = coords(j)
        a = piece(j, add(p, 2), q)
        w_arrived(j, 1, 1)
        w_send(j, QA + 3, a, a, 0, 1)
        w_send(j, QB + 3, a, a, 0, 3)

    order = (0, 3, 1, 2)

    def relay(j, i):
        p, q = coords(j)
        a = piece(j, add(p, order[i]), add(q, 3))
        b = piece(j, add(p, order[i]), add(q, 1))
        w_send(j, RA + i, a.at[lower], a.at[lower], 0, 1)
        w_send(j, RB + i, b.at[upper], b.at[upper], 0, 3)

    def stage4(j):
        w_arrived(j, 2, 6)
        for i in range(3):
            relay(j, i)

    def stage5(j):
        w_arrived(j, 3, 2)
        relay(j, 3)

    def stage6(j):
        w_arrived(j, 4, 4)
    stage1(0)
    stage1(1)
    load_emb.wait()

    def norm_rows(b, carry):
        rows = pl.ds(pl.multiple_of(b * 32, 32), 32)
        values = emb[rows, :].astype(F32)
        inv = lax.rsqrt(jnp.mean(values * values, axis=-1, keepdims=True) + 1e-06)
        normed[rows, :] = (values * inv * gain_ref[...]).astype(BF16)
        return carry
    lax.fori_loop(0, 4, norm_rows, 0)
    arrived(ids.at[chip, 1 - k], ir_sem)
    for d in chips:
        send(ids.at[chip], ids.at[chip], i_s, i_r, chip_dev(*d))
    lax.fori_loop(4, 16, norm_rows, 0)
    table = dot_t(sel[...], normed[...]).astype(BF16)
    tab[0 : 3 * CH, :] = table[:, 0:256]
    tab[3 * CH : 6 * CH, :] = table[:, 256:512]
    stage2(0)
    stage2(1)

    own_hot = lax.broadcasted_iota(jnp.int32, (VOCAB, 128), 0) == ids_ref[...]
    own_hot = jnp.where(own_hot, 1.0, 0.0).astype(F32).T.astype(BF16)
    resid[...] = jnp.dot(own_hot, emb[...], preferred_element_type=F32).astype(BF16)
    arrived(ids.at[pl.ds(0, 63)], i_r)

    lane = lax.broadcasted_iota(jnp.int32, (3 * CH, 128), 1).astype(F32).astype(BF16)
    not_first, not_two = lane >= 1, lane >= 2
    none = jnp.zeros((3 * CH, 128), BF16)
    vocab = lax.broadcasted_iota(jnp.int32, (256, 128), 0).astype(F32).astype(BF16)
    one, zero = jnp.ones((256, 128), BF16), jnp.zeros((256, 128), BF16)

    def mix_window(src_line, zz, h):
        hots, highs = [], []
        for b in range(4):
            row = ids[src_line * 4 + h * 2 + b // 2, b % 2]
            low = jnp.broadcast_to((row & 255).astype(F32).astype(BF16), (256, 128))
            hots.append(jnp.where(vocab == low, one, zero))
            highs.append(row >> 8)
        both = jnp.dot(tab[...], jnp.concatenate(hots, axis=1), preferred_element_type=F32)
        n = zz * 2 + h
        last1 = last2 = none
        for b in range(4):
            cols = slice(b * 128, (b + 1) * 128)
            now = jnp.where(highs[b] == 1, both[3 * CH :, cols], both[: 3 * CH, cols])
            packed = now.astype(BF16)
            roll1, roll2 = pltpu.roll(packed, 1, 1), pltpu.roll(packed, 2, 1)
            back1 = jnp.where(not_first, roll1, last1)
            back2 = jnp.where(not_two, roll2, last2)
            last1, last2 = roll1, roll2
            feat = tapb[0] * now + tapb[1] * back1.astype(F32) + tapb[2] * back2.astype(F32)
            pr = (feat[CH : 2 * CH] * feat[2 * CH :]).astype(BF16)
            for g in range(2):
                rows = slice(g * GROUP, (g + 1) * GROUP)
                qf[g, n, :, cols] = feat[rows]
                prod[g, n, :, cols] = pr[rows]

    def mix_rows(yy):
        def one_line(zz, carry):
            for h in range(2):
                mix_window(yy * 4 + zz, zz, h)
            return carry

        lax.fori_loop(0, 4, one_line, 0)
        for g in range(2):
            p = prod[g].reshape(128, LEN)
            first = jnp.dot(p[:, :256], toep[g, 128:], preferred_element_type=F32)
            second = jnp.dot(p[:, 128:], toep[g], preferred_element_type=F32)
            filt = jnp.concatenate([first, second], axis=1).reshape(8, GROUP, LEN)
            for n in range(8):
                gated = (qf[g, n] * filt[n]).astype(BF16)
                for b in range(4):
                    lanes = ((b % 2) * 4 + (n % 2) * 2 + b // 2) * 128
                    gsend[yy * 4 + n // 2, g * GROUP : (g + 1) * GROUP, lanes : lanes + 128] = (
                        gated[:, b * 128 : (b + 1) * 128]
                    )

    my_rows = pl.ds(pl.multiple_of(k * CH, CH), CH)
    sib_rows = pl.ds(pl.multiple_of((1 - k) * CH, CH), CH)

    half_lanes = (pl.ds(0, LEN), pl.ds(LEN, LEN))

    def scatter(dy, t):
        yy = add(y, dy)
        for dz in range(4):
            if (dy, dz) == (0, 0):
                continue
            send(gsend.at[yy * 4 + add(z, dz), :, half_lanes[t]],
                 gath.at[line, my_rows, half_lanes[t]],
                 g_s, g_r.at[t, dy], plane_dev(dy, dz))

    polls = {2: lambda: (stage3(0),stage3(1),),1: lambda: (stage4(0),stage4(1),),3: lambda: (stage5(0),stage5(1),),0: lambda: (stage1(2),stage1(3),)}
    for dy in (2, 1, 3, 0):
        mix_rows(add(y, dy))
        scatter(dy, 0)
        polls[dy]()

    own_g = pltpu.make_async_copy(gsend.at[line], gath.at[line, my_rows], gl_sem)
    own_g.start()

    def row_of(dy):
        return pl.ds(pl.multiple_of(add(y, 4 - dy) * 4, 4), 4)

    def hand_over(t):
        lanes = half_lanes[t]
        for dy in (2, 1, 3, 0):
            arrived(gath.at[pl.ds(0, 4 if dy else 3), my_rows, lanes], g_r.at[t, dy])
            if t == 0 and dy == 0:
                own_g.wait()
            there = gath.at[row_of(dy), my_rows, lanes]
            send(there, there, b_s, b_r.at[t, dy], line_dev(0, 1))

    def fill_lhs(t):
        lanes = half_lanes[t]
        for dy in (2, 1, 3, 0):
            sy = add(y, 4 - dy)
            arrived(gath.at[row_of(dy), sib_rows, lanes], b_r.at[t, dy])
            for pair in range(2):
                block = jnp.concatenate(
                    [gath[sy * 4 + 2 * pair, :, lanes], gath[sy * 4 + 2 * pair + 1, :, lanes]],
                    axis=0,
                )
                cols = pl.multiple_of(sy * 256 + pair * 128, 128)
                lhs[t * LEN : (t + 1) * LEN, pl.ds(cols, 128)] = block.T

    def w_ready(j):
        stage6(j)

    def multiply(t, j):

        def times(dx):
            w = wbuf[j * 16 : (j + 1) * 16].reshape(16 * 64, CW)
            rows = pl.ds(pl.multiple_of(t * LEN + add(x, dx) * 128, 128), 128)
            return jnp.dot(lhs[rows, :], w, preferred_element_type=F32)

        far = times(2).astype(BF16)
        for side, dx in ((0, 1), (1, 3)):
            opp_s[j, t, side] = far[:, side * 256 : (side + 1) * 256]
            send(opp_s.at[j, t, side], opp_r.at[j, t, side],
                 o_s, o_r.at[j, t], line_dev(dx, 0))
        part[j, t, 0] = times(1)
        part[j, t, 1] = times(3)
        mine[t, j, k] = times(0).astype(BF16)
        if t == 1:
            send(mine.at[1 - k, j, k], mine.at[1 - k, j, k], m_s, m_r.at[j], line_dev(0, 1))

    def pass_on(t, j):
        arrived(opp_r.at[j, t], o_r.at[j, t])
        for side, dx in ((0, 1), (1, 3)):
            half = slice(side * 256, (side + 1) * 256)
            rest = slice((1 - side) * 256, (2 - side) * 256)
            fin_s[j, t, side, :, rest] = part[j, t, side, :, rest].astype(BF16)
            fin_s[j, t, side, :, half] = (
                part[j, t, side, :, half] + opp_r[j, t, side].astype(F32)
            ).astype(BF16)
            send(fin_s.at[j, t, side], fin_r.at[j, side, k],
                 f_s, f_r.at[j], dev(add(x, dx), y, z, t))

    def finish(j):
        arrived(mine.at[k, j, 1 - k], m_r.at[j])
        arrived(fin_r.at[j], f_r.at[j])
        for h in range(2):
            cols = slice(h * CHUNKS * CW + j * CW, h * CHUNKS * CW + (j + 1) * CW)
            total = (
                fin_r[j, 0, h].astype(F32) + fin_r[j, 1, h].astype(F32)
                + mine[k, j, h].astype(F32) + resid[:, cols].astype(F32)
            )
            outb[:, cols] = total.astype(BF16)
            pltpu.make_async_copy(outb.at[:, cols], out_ref.at[:, cols], out_sem).start()
    hand_over(0)
    for dy in (2, 1, 3, 0):
        scatter(dy, 1)
    fill_lhs(0)
    pltpu.make_async_copy(wbuf.at[pl.ds(0, CHUNKS)], wbuf.at[pl.ds(0, CHUNKS)], wl_sem).wait()
    w_ready(0)
    multiply(0, 0)
    w_ready(1)
    multiply(0, 1)
    pass_on(0, 0)
    pass_on(0, 1)
    hand_over(1)
    stage2(2)
    stage2(3)
    fill_lhs(1)
    multiply(1, 0)
    multiply(1, 1)
    stage3(2)
    stage3(3)
    pass_on(1, 0)
    stage4(2)
    stage4(3)
    pass_on(1, 1)
    stage5(2)
    stage5(3)
    w_ready(2)
    multiply(0, 2)
    multiply(1, 2)
    w_ready(3)
    multiply(0, 3)
    pass_on(0, 2)
    multiply(1, 3)
    pass_on(1, 2)
    pass_on(0, 3)
    pass_on(1, 3)
    for j in range(CHUNKS):
        finish(j)
    pltpu.make_async_copy(outb, out_ref, out_sem).wait()
    all_sent(ids.at[chip, k], is_sem)
    all_sent(ids.at[pl.ds(0, 63)], i_s)
    all_sent(wbuf.at[pl.ds(0, 15 * CHUNKS)], w_s)
    all_sent(gath.at[pl.ds(0, 15), pl.ds(0, CH), :], g_s)
    all_sent(gath.at[:, pl.ds(0, CH), :], b_s)
    all_sent(opp_s, o_s)
    all_sent(fin_s, f_s)
    all_sent(mine.at[0, :, 0], m_s)


def per_device(token_ids, embedding, norm_gain, in_proj, short_taps, conv_taps, out_proj):
    vmem = pl.BlockSpec(memory_space=pltpu.VMEM)
    hbm = pl.BlockSpec(memory_space=pl.ANY)
    dma = pltpu.SemaphoreType.DMA
    out = pl.pallas_call(
        kernel,
        out_shape=jax.ShapeDtypeStruct((128, D), BF16),
        in_specs=[vmem, vmem, vmem, vmem, hbm, hbm, hbm],
        out_specs=hbm,
        scratch_shapes=[
            pltpu.VMEM((VOCAB, D), BF16),
            pltpu.VMEM((3, D, 128), BF16),
            pltpu.VMEM((VOCAB, D), BF16),
            pltpu.VMEM((3 * CH, D), BF16),
            pltpu.VMEM((6 * CH, 256), BF16),
            pltpu.VMEM((64, 2, 1, 128), jnp.int32),
            pltpu.VMEM((128, 128), F32),
            pltpu.VMEM((SHORT, 3 * CH, 128), F32),
            pltpu.VMEM((2, 384, 256), BF16),
            pltpu.VMEM((2, 8, GROUP, LEN), BF16),
            pltpu.VMEM((2, 8, GROUP, LEN), F32),
            pltpu.VMEM((16, CH, 2 * LEN), BF16),
            pltpu.VMEM((16, 2 * CH, 2 * LEN), BF16),
            pltpu.VMEM((2 * LEN, 1024), BF16),
            pltpu.VMEM((CHUNKS * 16, 64, CW), BF16),
            pltpu.VMEM((CHUNKS, 2, 2, 128, 256), BF16),
            pltpu.VMEM((CHUNKS, 2, 2, 128, 256), BF16),
            pltpu.VMEM((CHUNKS, 2, 2, 128, CW), F32),
            pltpu.VMEM((CHUNKS, 2, 2, 128, CW), BF16),
            pltpu.VMEM((CHUNKS, 2, 2, 128, CW), BF16),
            pltpu.VMEM((2, CHUNKS, 2, 128, CW), BF16),
            pltpu.VMEM((128, D), BF16),
            pltpu.VMEM((128, D), BF16),
            dma((3,)), dma((N_ONE,)), dma((CHUNKS, 5)), dma((2, 4)), dma((2, 4)),
            dma((CHUNKS, 2)), dma((CHUNKS,)), dma((CHUNKS,)),
        ],
        compiler_params=pltpu.CompilerParams(
            collective_id=0, has_side_effects=True, vmem_limit_bytes=60 * 1024 * 1024
        ),
        name="mixer",
    )(token_ids, norm_gain.reshape(1, D), short_taps, conv_taps, embedding, in_proj, out_proj)
    return out[None]


def solution(mesh):
    return jax.shard_map(
        per_device,
        mesh=mesh,
        in_specs=(
            P("fsdp", "ctx"),
            P(),
            P(),
            P(None, None, "fsdp"),
            P(None, None, "fsdp"),
            P("fsdp", None),
            P("fsdp", None),
        ),
        out_specs=P("fsdp", "ctx", None),
        check_vma=False,
    )
```

```python
import jax
import jax.numpy as jnp
from jax import lax
from jax.experimental import pallas as pl
from jax.experimental.pallas import tpu as pltpu
from jax.sharding import PartitionSpec as P

GROUP = 16
TAPS = 128
SHORT = 3
VOCAB = 512
D = 4096
LEN = 512
CH = 32
CHUNKS = 4
CW = 512
F32 = jnp.float32
BF16 = jnp.bfloat16
MESH = pl.DeviceIdType.MESH

PA, PB, PH0, PH1, QA, QB, RA, RB = 0, 1, 2, 3, 4, 8, 12, 16
ROUND = {PA: 0, PB: 0, PH0: 1, PH1: 1, QA: 2, QA + 1: 2, QA + 2: 2, QA + 3: 3,
         QB: 2, QB + 1: 2, QB + 2: 2, QB + 3: 3, **{RA + i: 4 for i in range(8)}}
N_ONE = 12


def dot_t(a, b):
    return lax.dot_general(a, b, (((1,), (1,)), ((), ())), preferred_element_type=F32)


def kernel(
    ids_in, gain_in, staps_in, ctaps_in, emb_ref, inp_ref, op_ref, out_ref,
    ids_ref, gain_ref, staps_ref, ctaps_ref,
    emb, inp, normed, sel, tab, ids, taps, tapb, toep, prod, qf, gsend, gath, lhs, wbuf,
    opp_s, opp_r, part, fin_s, fin_r, mine, resid,
    ld_sem, one_sem, w_r, g_r, b_r, o_r, f_r, m_r,
):
    wl_sem, gl_sem, is_sem, ir_sem, i_s, i_r, w_s, g_s, b_s, o_s, f_s, m_s = (
        one_sem.at[i] for i in range(N_ONE)
    )
    f = lax.axis_index("fsdp")
    c = lax.axis_index("ctx")
    xh, y, z = f // 16, (f // 4) % 4, f % 4
    xl, k = c // 2, c % 2
    x = xh * 2 + xl
    line = y * 4 + z

    def dev(xx, yy, zz, kk):
        return {"fsdp": (xx // 2) * 16 + yy * 4 + zz, "ctx": (xx % 2) * 2 + kk}

    def add(a, n):
        return (a + n) % 4

    def remote(src, dst, ssem, rsem, target):
        return pltpu.make_async_remote_copy(
            src_ref=src, dst_ref=dst, send_sem=ssem, recv_sem=rsem,
            device_id=target, device_id_type=MESH,
        )

    here = {"fsdp": f, "ctx": c}
    def send(src, dst, ssem, rsem, target):
        remote(src, dst, ssem, rsem, target).start()

    def arrived(dst, rsem):
        remote(dst, dst, rsem, rsem, here).wait_recv()

    def all_sent(src, ssem):
        remote(src, src, ssem, ssem, here).wait_send()

    def line_dev(dx, dk):
        return dev(add(x, dx), y, z, (k + dk) % 2)

    def plane_dev(dy, dz):
        return dev(x, add(y, dy), add(z, dz), k)

    chip = line * 4 + x

    small = []
    for i, (src, dst) in enumerate((
        (ids_in, ids_ref), (staps_in, staps_ref), (ctaps_in, ctaps_ref), (gain_in, gain_ref)
    )):
        small.append(pltpu.make_async_copy(src, dst, ld_sem.at[2 + i]))
        small[-1].start()
    load_inp = pltpu.make_async_copy(inp_ref, inp, ld_sem.at[0])
    load_inp.start()
    load_emb = pltpu.make_async_copy(emb_ref, emb, ld_sem.at[1])
    load_emb.start()

    def w_source(j):
        cols = pl.multiple_of(k * (CHUNKS * CW) + j * CW, CW)
        return op_ref.at[pl.ds(pl.multiple_of(xl * 64, 64), 64), pl.ds(cols, CW)]

    for j in range(CHUNKS):
        pltpu.make_async_copy(w_source(j), wbuf.at[j * 16 + line], wl_sem).start()
    own_ids = pltpu.make_async_copy(ids_in, ids.at[chip, k], ld_sem.at[6])
    own_ids.start()

    xs = [add(x, i) for i in range(4)]
    ctxs = [(xx % 2) * 2 + k for xx in xs]
    fsdps = [(xx // 2) * 16 for xx in xs]
    rows = [add(y, i) * 4 for i in range(4)]
    cols = [add(z, i) for i in range(4)]
    chips = [(dx, dy, dz) for dy in range(4) for dz in range(4) for dx in range(4)][1:]

    def chip_dev(dx, dy, dz):
        return {"fsdp": fsdps[dx] + rows[dy] + cols[dz], "ctx": ctxs[dx]}

    barrier = pltpu.get_barrier_semaphore()
    for dx in (0, 1, 3):
        pl.semaphore_signal(barrier, inc=1, device_id=line_dev(dx, 1), device_id_type=MESH)
    for d in chips:
        pl.semaphore_signal(barrier, inc=1, device_id=chip_dev(*d), device_id_type=MESH)
    for copy in small:
        copy.wait()
    staps = jnp.concatenate(
        [staps_ref[j, :, :] for j in range(SHORT)] + [jnp.zeros((128 - 9, 128), F32)], axis=0
    )
    taps[...] = staps.T
    ch0 = pl.multiple_of(c * CH, CH)
    my_taps = taps[pl.ds(ch0, CH), :]
    for j in range(SHORT):
        for i in range(3):
            tapb[j, i * CH : (i + 1) * CH, :] = jnp.broadcast_to(
                my_taps[:, 3 * j + i : 3 * j + i + 1], (CH, 128)
            )

    all_taps = ctaps_ref[...].astype(F32)
    rows8 = lax.broadcasted_iota(jnp.int32, (8, 128), 0)
    for g in range(2):
        row = jnp.sum(jnp.where(rows8 == 2 * c + g, all_taps, 0.0), axis=0, keepdims=True)
        base = jnp.concatenate([row, jnp.zeros((1, 384), F32)], axis=1)
        base = jnp.broadcast_to(base, (384, 512))
        band = pltpu.roll(base, 384, 1, stride=1, stride_axis=0)
        toep[g] = band[:, :256].astype(BF16)

    load_inp.wait()
    pick = (
        lax.broadcasted_iota(jnp.int32, (CH, 128), 1)
        == lax.broadcasted_iota(jnp.int32, (CH, 128), 0) + ch0
    )
    pick = jnp.where(pick, 1.0, 0.0).astype(BF16)
    for i in range(3):
        for d0 in range(0, D, 1024):
            sel[i * CH : (i + 1) * CH, d0 : d0 + 1024] = dot_t(
                pick, inp[i, d0 : d0 + 1024, :]
            ).astype(BF16)
    pl.semaphore_wait(barrier, 66)
    own_ids.wait()
    send(ids_ref, ids.at[chip, k], is_sem, ir_sem, line_dev(0, 1))

    def piece(j, p, q):
        return wbuf.at[j * 16 + (p * 4 + q if j % 2 == 0 else q * 4 + p)]

    def coords(j):
        return (y, z) if j % 2 == 0 else (z, y)

    def w_dev(j, dp, dq):
        return plane_dev(dp, dq) if j % 2 == 0 else plane_dev(dq, dp)

    def w_send(j, role, src, dst, dp, dq):
        send(src, dst, w_s, w_r.at[j, ROUND[role]], w_dev(j, dp, dq))

    def w_arrived(j, n, pieces):
        arrived(wbuf.at[pl.ds(j * 16, pieces)], w_r.at[j, n])

    lower, upper = pl.ds(0, 32), pl.ds(32, 32)

    def stage1(j):
        p, q = coords(j)
        src, dst = w_source(j), piece(j, p, q)
        w_send(j, PA, src, dst, 1, 0)
        w_send(j, PB, src, dst, 3, 0)
        w_send(j, QA, src, dst, 0, 1)
        w_send(j, QB, src, dst, 0, 3)

    def stage2(j):
        p, q = coords(j)
        a, b = piece(j, add(p, 3), q), piece(j, add(p, 1), q)
        w_arrived(j, 0, 2)
        w_send(j, PH0, a.at[lower], a.at[lower], 1, 0)
        w_send(j, PH1, b.at[upper], b.at[upper], 3, 0)
        w_send(j, QA + 1, a, a, 0, 1)
        w_send(j, QB + 1, a, a, 0, 3)
        w_send(j, QA + 2, b, b, 0, 1)
        w_send(j, QB + 2, b, b, 0, 3)

    def stage3(j):
        p, q = coords(j)
        a = piece(j, add(p, 2), q)
        w_arrived(j, 1, 1)
        w_send(j, QA + 3, a, a, 0, 1)
        w_send(j, QB + 3, a, a, 0, 3)

    order = (0, 3, 1, 2)

    def relay(j, i):
        p, q = coords(j)
        a = piece(j, add(p, order[i]), add(q, 3))
        b = piece(j, add(p, order[i]), add(q, 1))
        w_send(j, RA + i, a.at[lower], a.at[lower], 0, 1)
        w_send(j, RB + i, b.at[upper], b.at[upper], 0, 3)

    def stage4(j):
        w_arrived(j, 2, 6)
        for i in range(3):
            relay(j, i)

    def stage5(j):
        w_arrived(j, 3, 2)
        relay(j, 3)

    def stage6(j):
        w_arrived(j, 4, 4)
    stage1(0)
    stage1(1)
    load_emb.wait()

    def norm_rows(b, carry):
        rows = pl.ds(pl.multiple_of(b * 32, 32), 32)
        values = emb[rows, :].astype(F32)
        inv = lax.rsqrt(jnp.mean(values * values, axis=-1, keepdims=True) + 1e-06)
        normed[rows, :] = (values * inv * gain_ref[...]).astype(BF16)
        return carry
    lax.fori_loop(0, 4, norm_rows, 0)
    arrived(ids.at[chip, 1 - k], ir_sem)
    for d in chips:
        send(ids.at[chip], ids.at[chip], i_s, i_r, chip_dev(*d))
    lax.fori_loop(4, 16, norm_rows, 0)
    table = dot_t(sel[...], normed[...]).astype(BF16)
    tab[0 : 3 * CH, :] = table[:, 0:256]
    tab[3 * CH : 6 * CH, :] = table[:, 256:512]
    stage2(0)
    stage2(1)

    own_hot = lax.broadcasted_iota(jnp.int32, (VOCAB, 128), 0) == ids_ref[...]
    own_hot = jnp.where(own_hot, 1.0, 0.0).astype(F32).T.astype(BF16)
    resid[...] = jnp.dot(own_hot, emb[...], preferred_element_type=F32).astype(BF16)
    arrived(ids.at[pl.ds(0, 63)], i_r)

    lane = lax.broadcasted_iota(jnp.int32, (3 * CH, 128), 1).astype(F32).astype(BF16)
    not_first, not_two = lane >= 1, lane >= 2
    none = jnp.zeros((3 * CH, 128), BF16)
    vocab = lax.broadcasted_iota(jnp.int32, (256, 128), 0).astype(F32).astype(BF16)
    one, zero = jnp.ones((256, 128), BF16), jnp.zeros((256, 128), BF16)

    def mix_window(src_line, zz, h):
        hots, highs = [], []
        for b in range(4):
            row = ids[src_line * 4 + h * 2 + b // 2, b % 2]
            low = jnp.broadcast_to((row & 255).astype(F32).astype(BF16), (256, 128))
            hots.append(jnp.where(vocab == low, one, zero))
            highs.append(row >> 8)
        both = jnp.dot(tab[...], jnp.concatenate(hots, axis=1), preferred_element_type=F32)
        n = zz * 2 + h
        last1 = last2 = none
        for b in range(4):
            cols = slice(b * 128, (b + 1) * 128)
            now = jnp.where(highs[b] == 1, both[3 * CH :, cols], both[: 3 * CH, cols])
            packed = now.astype(BF16)
            roll1, roll2 = pltpu.roll(packed, 1, 1), pltpu.roll(packed, 2, 1)
            back1 = jnp.where(not_first, roll1, last1)
            back2 = jnp.where(not_two, roll2, last2)
            last1, last2 = roll1, roll2
            feat = tapb[0] * now + tapb[1] * back1.astype(F32) + tapb[2] * back2.astype(F32)
            pr = (feat[CH : 2 * CH] * feat[2 * CH :]).astype(BF16)
            for g in range(2):
                rows = slice(g * GROUP, (g + 1) * GROUP)
                qf[g, n, :, cols] = feat[rows]
                prod[g, n, :, cols] = pr[rows]

    def mix_rows(yy):
        def one_line(zz, carry):
            for h in range(2):
                mix_window(yy * 4 + zz, zz, h)
            return carry

        lax.fori_loop(0, 4, one_line, 0)
        for g in range(2):
            p = prod[g].reshape(128, LEN)
            first = jnp.dot(p[:, :256], toep[g, 128:], preferred_element_type=F32)
            second = jnp.dot(p[:, 128:], toep[g], preferred_element_type=F32)
            filt = jnp.concatenate([first, second], axis=1).reshape(8, GROUP, LEN)
            for n in range(8):
                gated = (qf[g, n] * filt[n]).astype(BF16)
                for b in range(4):
                    lanes = ((b % 2) * 4 + (n % 2) * 2 + b // 2) * 128
                    gsend[yy * 4 + n // 2, g * GROUP : (g + 1) * GROUP, lanes : lanes + 128] = (
                        gated[:, b * 128 : (b + 1) * 128]
                    )

    my_rows = pl.ds(pl.multiple_of(k * CH, CH), CH)
    sib_rows = pl.ds(pl.multiple_of((1 - k) * CH, CH), CH)

    half_lanes = (pl.ds(0, LEN), pl.ds(LEN, LEN))

    def scatter(dy, t):
        yy = add(y, dy)
        for dz in range(4):
            if (dy, dz) == (0, 0):
                continue
            send(gsend.at[yy * 4 + add(z, dz), :, half_lanes[t]],
                 gath.at[line, my_rows, half_lanes[t]],
                 g_s, g_r.at[t, dy], plane_dev(dy, dz))

    polls = {2: lambda: (None,),1: lambda: (stage3(0),stage3(1),),3: lambda: (stage4(0),stage4(1),),0: lambda: (stage5(0),stage5(1),)}
    for dy in (2, 1, 3, 0):
        mix_rows(add(y, dy))
        scatter(dy, 0)
        polls[dy]()

    own_g = pltpu.make_async_copy(gsend.at[line], gath.at[line, my_rows], gl_sem)
    own_g.start()

    def row_of(dy):
        return pl.ds(pl.multiple_of(add(y, 4 - dy) * 4, 4), 4)

    def hand_over(t):
        lanes = half_lanes[t]
        for dy in (2, 1, 3, 0):
            arrived(gath.at[pl.ds(0, 4 if dy else 3), my_rows, lanes], g_r.at[t, dy])
            if t == 0 and dy == 0:
                own_g.wait()
            there = gath.at[row_of(dy), my_rows, lanes]
            send(there, there, b_s, b_r.at[t, dy], line_dev(0, 1))

    def fill_lhs(t):
        lanes = half_lanes[t]
        for dy in (2, 1, 3, 0):
            sy = add(y, 4 - dy)
            arrived(gath.at[row_of(dy), sib_rows, lanes], b_r.at[t, dy])
            for pair in range(2):
                block = jnp.concatenate(
                    [gath[sy * 4 + 2 * pair, :, lanes], gath[sy * 4 + 2 * pair + 1, :, lanes]],
                    axis=0,
                )
                cols = pl.multiple_of(sy * 256 + pair * 128, 128)
                lhs[t * LEN : (t + 1) * LEN, pl.ds(cols, 128)] = block.T

    def w_ready(j):
        stage6(j)

    def multiply(t, j):

        def times(dx):
            w = wbuf[j * 16 : (j + 1) * 16].reshape(16 * 64, CW)
            rows = pl.ds(pl.multiple_of(t * LEN + add(x, dx) * 128, 128), 128)
            return jnp.dot(lhs[rows, :], w, preferred_element_type=F32)

        far = times(2).astype(BF16)
        for side, dx in ((0, 1), (1, 3)):
            opp_s[j, t, side] = far[:, side * 256 : (side + 1) * 256]
            send(opp_s.at[j, t, side], opp_r.at[j, t, side],
                 o_s, o_r.at[j, t], line_dev(dx, 0))
        part[j, t, 0] = times(1)
        part[j, t, 1] = times(3)
        mine[t, j, k] = times(0).astype(BF16)
        if t == 1:
            send(mine.at[1 - k, j, k], mine.at[1 - k, j, k], m_s, m_r.at[j], line_dev(0, 1))

    def pass_on(t, j):
        arrived(opp_r.at[j, t], o_r.at[j, t])
        for side, dx in ((0, 1), (1, 3)):
            half = slice(side * 256, (side + 1) * 256)
            rest = slice((1 - side) * 256, (2 - side) * 256)
            fin_s[j, t, side, :, rest] = part[j, t, side, :, rest].astype(BF16)
            fin_s[j, t, side, :, half] = (
                part[j, t, side, :, half] + opp_r[j, t, side].astype(F32)
            ).astype(BF16)
            send(fin_s.at[j, t, side], fin_r.at[j, side, k],
                 f_s, f_r.at[j], dev(add(x, dx), y, z, t))

    def finish(j):
        arrived(mine.at[k, j, 1 - k], m_r.at[j])
        arrived(fin_r.at[j], f_r.at[j])
        for h in range(2):
            cols = slice(h * CHUNKS * CW + j * CW, h * CHUNKS * CW + (j + 1) * CW)
            total = (
                fin_r[j, 0, h].astype(F32) + fin_r[j, 1, h].astype(F32)
                + mine[k, j, h].astype(F32) + resid[:, cols].astype(F32)
            )
            out_ref[:, cols] = total.astype(BF16)
    hand_over(0)
    for dy in (2, 1, 3, 0):
        scatter(dy, 1)
    stage1(2)
    stage1(3)
    fill_lhs(0)
    pltpu.make_async_copy(wbuf.at[pl.ds(0, CHUNKS)], wbuf.at[pl.ds(0, CHUNKS)], wl_sem).wait()
    w_ready(0)
    multiply(0, 0)
    w_ready(1)
    multiply(0, 1)
    pass_on(0, 0)
    pass_on(0, 1)
    hand_over(1)
    stage2(2)
    stage2(3)
    fill_lhs(1)
    multiply(1, 0)
    multiply(1, 1)
    stage3(2)
    stage3(3)
    pass_on(1, 0)
    stage4(2)
    stage4(3)
    pass_on(1, 1)
    stage5(2)
    stage5(3)
    w_ready(2)
    multiply(0, 2)
    multiply(1, 2)
    w_ready(3)
    multiply(0, 3)
    pass_on(0, 2)
    multiply(1, 3)
    pass_on(1, 2)
    pass_on(0, 3)
    pass_on(1, 3)
    for j in range(CHUNKS):
        finish(j)
    all_sent(ids.at[chip, k], is_sem)
    all_sent(ids.at[pl.ds(0, 63)], i_s)
    all_sent(wbuf.at[pl.ds(0, 15 * CHUNKS)], w_s)
    all_sent(gath.at[pl.ds(0, 15), pl.ds(0, CH), :], g_s)
    all_sent(gath.at[:, pl.ds(0, CH), :], b_s)
    all_sent(opp_s, o_s)
    all_sent(fin_s, f_s)
    all_sent(mine.at[0, :, 0], m_s)


def per_device(token_ids, embedding, norm_gain, in_proj, short_taps, conv_taps, out_proj):
    vmem = pl.BlockSpec(memory_space=pltpu.VMEM)
    hbm = pl.BlockSpec(memory_space=pltpu.HBM)
    dma = pltpu.SemaphoreType.DMA
    out = pl.pallas_call(
        kernel,
        out_shape=jax.ShapeDtypeStruct((128, D), BF16),
        in_specs=[hbm] * 7,
        out_specs=vmem,
        scratch_shapes=[
            pltpu.VMEM((1, 128), jnp.int32),
            pltpu.VMEM((1, D), F32),
            pltpu.VMEM((SHORT, 3, 128), F32),
            pltpu.VMEM((8, 128), BF16),
            pltpu.VMEM((VOCAB, D), BF16),
            pltpu.VMEM((3, D, 128), BF16),
            pltpu.VMEM((VOCAB, D), BF16),
            pltpu.VMEM((3 * CH, D), BF16),
            pltpu.VMEM((6 * CH, 256), BF16),
            pltpu.VMEM((64, 2, 1, 128), jnp.int32),
            pltpu.VMEM((128, 128), F32),
            pltpu.VMEM((SHORT, 3 * CH, 128), F32),
            pltpu.VMEM((2, 384, 256), BF16),
            pltpu.VMEM((2, 8, GROUP, LEN), BF16),
            pltpu.VMEM((2, 8, GROUP, LEN), F32),
            pltpu.VMEM((16, CH, 2 * LEN), BF16),
            pltpu.VMEM((16, 2 * CH, 2 * LEN), BF16),
            pltpu.VMEM((2 * LEN, 1024), BF16),
            pltpu.VMEM((CHUNKS * 16, 64, CW), BF16),
            pltpu.VMEM((CHUNKS, 2, 2, 128, 256), BF16),
            pltpu.VMEM((CHUNKS, 2, 2, 128, 256), BF16),
            pltpu.VMEM((CHUNKS, 2, 2, 128, CW), F32),
            pltpu.VMEM((CHUNKS, 2, 2, 128, CW), BF16),
            pltpu.VMEM((CHUNKS, 2, 2, 128, CW), BF16),
            pltpu.VMEM((2, CHUNKS, 2, 128, CW), BF16),
            pltpu.VMEM((128, D), BF16),
            dma((7,)), dma((N_ONE,)), dma((CHUNKS, 5)), dma((2, 4)), dma((2, 4)),
            dma((CHUNKS, 2)), dma((CHUNKS,)), dma((CHUNKS,)),
        ],
        compiler_params=pltpu.CompilerParams(
            collective_id=0, has_side_effects=True, vmem_limit_bytes=46 * 1024 * 1024
        ),
        name="mixer",
    )(*(
        pltpu.with_memory_space_constraint(v, pltpu.HBM)
        for v in (token_ids, norm_gain.reshape(1, D), short_taps, conv_taps, embedding,
                  in_proj, out_proj)
    ))
    return out[None]


def solution(mesh):
    return jax.shard_map(
        per_device,
        mesh=mesh,
        in_specs=(
            P("fsdp", "ctx"),
            P(),
            P(),
            P(None, None, "fsdp"),
            P(None, None, "fsdp"),
            P("fsdp", None),
            P("fsdp", None),
        ),
        out_specs=P("fsdp", "ctx", None),
        check_vma=False,
    )
```

```python
import jax
import jax.numpy as jnp
from jax import lax
from jax.experimental import pallas as pl
from jax.experimental.pallas import tpu as pltpu
from jax.sharding import PartitionSpec as P

GROUP = 16
TAPS = 128
SHORT = 3
VOCAB = 512
D = 4096
LEN = 512
CH = 32
CHUNKS = 4
CW = 512
F32 = jnp.float32
BF16 = jnp.bfloat16
MESH = pl.DeviceIdType.MESH

PA, PB, PH0, PH1, QA, QB, RA, RB = 0, 1, 2, 3, 4, 8, 12, 16
ROUND = {PA: 0, PB: 0, PH0: 1, PH1: 1, QA: 2, QA + 1: 2, QA + 2: 2, QA + 3: 3,
         QB: 2, QB + 1: 2, QB + 2: 2, QB + 3: 3, **{RA + i: 4 for i in range(8)}}
N_ONE = 12


def dot_t(a, b):
    return lax.dot_general(a, b, (((1,), (1,)), ((), ())), preferred_element_type=F32)


def kernel(
    ids_in, gain_in, staps_in, ctaps_in, emb_ref, inp_ref, op_ref, out_ref,
    ids_ref, gain_ref, staps_ref, ctaps_ref,
    emb, inp, normed, sel, tab, ids, taps, tapb, toep, prod, qf, gsend, gath, lhs, wbuf,
    opp_s, opp_r, part, fin_s, fin_r, mine, resid,
    ld_sem, one_sem, w_r, g_r, b_r, o_r, f_r, m_r,
):
    wl_sem, gl_sem, is_sem, ir_sem, i_s, i_r, w_s, g_s, b_s, o_s, f_s, m_s = (
        one_sem.at[i] for i in range(N_ONE)
    )
    f = lax.axis_index("fsdp")
    c = lax.axis_index("ctx")
    xh, y, z = f // 16, (f // 4) % 4, f % 4
    xl, k = c // 2, c % 2
    x = xh * 2 + xl
    line = y * 4 + z

    def dev(xx, yy, zz, kk):
        return {"fsdp": (xx // 2) * 16 + yy * 4 + zz, "ctx": (xx % 2) * 2 + kk}

    def add(a, n):
        return (a + n) % 4

    def remote(src, dst, ssem, rsem, target):
        return pltpu.make_async_remote_copy(
            src_ref=src, dst_ref=dst, send_sem=ssem, recv_sem=rsem,
            device_id=target, device_id_type=MESH,
        )

    here = {"fsdp": f, "ctx": c}
    def send(src, dst, ssem, rsem, target):
        remote(src, dst, ssem, rsem, target).start()

    def arrived(dst, rsem):
        remote(dst, dst, rsem, rsem, here).wait_recv()

    def all_sent(src, ssem):
        remote(src, src, ssem, ssem, here).wait_send()

    def line_dev(dx, dk):
        return dev(add(x, dx), y, z, (k + dk) % 2)

    def plane_dev(dy, dz):
        return dev(x, add(y, dy), add(z, dz), k)

    chip = line * 4 + x

    small = []
    for i, (src, dst) in enumerate((
        (ids_in, ids_ref), (staps_in, staps_ref), (ctaps_in, ctaps_ref), (gain_in, gain_ref)
    )):
        small.append(pltpu.make_async_copy(src, dst, ld_sem.at[2 + i]))
        small[-1].start()
    load_inp = pltpu.make_async_copy(inp_ref, inp, ld_sem.at[0])
    load_inp.start()
    load_emb = pltpu.make_async_copy(emb_ref, emb, ld_sem.at[1])
    load_emb.start()

    def w_source(j):
        cols = pl.multiple_of(k * (CHUNKS * CW) + j * CW, CW)
        return op_ref.at[pl.ds(pl.multiple_of(xl * 64, 64), 64), pl.ds(cols, CW)]

    for j in range(CHUNKS):
        pltpu.make_async_copy(w_source(j), wbuf.at[j * 16 + line], wl_sem).start()
    own_ids = pltpu.make_async_copy(ids_in, ids.at[chip, k], ld_sem.at[6])
    own_ids.start()

    xs = [add(x, i) for i in range(4)]
    ctxs = [(xx % 2) * 2 + k for xx in xs]
    fsdps = [(xx // 2) * 16 for xx in xs]
    rows = [add(y, i) * 4 for i in range(4)]
    cols = [add(z, i) for i in range(4)]
    chips = [(dx, dy, dz) for dy in range(4) for dz in range(4) for dx in range(4)][1:]

    def chip_dev(dx, dy, dz):
        return {"fsdp": fsdps[dx] + rows[dy] + cols[dz], "ctx": ctxs[dx]}

    barrier = pltpu.get_barrier_semaphore()
    for dx in (0, 1, 3):
        pl.semaphore_signal(barrier, inc=1, device_id=line_dev(dx, 1), device_id_type=MESH)
    for d in chips:
        pl.semaphore_signal(barrier, inc=1, device_id=chip_dev(*d), device_id_type=MESH)
    for copy in small:
        copy.wait()
    staps = jnp.concatenate(
        [staps_ref[j, :, :] for j in range(SHORT)] + [jnp.zeros((128 - 9, 128), F32)], axis=0
    )
    taps[...] = staps.T
    ch0 = pl.multiple_of(c * CH, CH)
    my_taps = taps[pl.ds(ch0, CH), :]
    for j in range(SHORT):
        for i in range(3):
            tapb[j, i * CH : (i + 1) * CH, :] = jnp.broadcast_to(
                my_taps[:, 3 * j + i : 3 * j + i + 1], (CH, 128)
            )

    all_taps = ctaps_ref[...].astype(F32)
    rows8 = lax.broadcasted_iota(jnp.int32, (8, 128), 0)
    for g in range(2):
        row = jnp.sum(jnp.where(rows8 == 2 * c + g, all_taps, 0.0), axis=0, keepdims=True)
        base = jnp.concatenate([row, jnp.zeros((1, 384), F32)], axis=1)
        base = jnp.broadcast_to(base, (384, 512))
        band = pltpu.roll(base, 384, 1, stride=1, stride_axis=0)
        toep[g] = band[:, :256].astype(BF16)

    load_inp.wait()
    pick = (
        lax.broadcasted_iota(jnp.int32, (CH, 128), 1)
        == lax.broadcasted_iota(jnp.int32, (CH, 128), 0) + ch0
    )
    pick = jnp.where(pick, 1.0, 0.0).astype(BF16)
    for i in range(3):
        for d0 in range(0, D, 1024):
            sel[i * CH : (i + 1) * CH, d0 : d0 + 1024] = dot_t(
                pick, inp[i, d0 : d0 + 1024, :]
            ).astype(BF16)
    pl.semaphore_wait(barrier, 66)
    own_ids.wait()
    send(ids_ref, ids.at[chip, k], is_sem, ir_sem, line_dev(0, 1))

    def piece(j, p, q):
        return wbuf.at[j * 16 + (p * 4 + q if j % 2 == 0 else q * 4 + p)]

    def coords(j):
        return (y, z) if j % 2 == 0 else (z, y)

    def w_dev(j, dp, dq):
        return plane_dev(dp, dq) if j % 2 == 0 else plane_dev(dq, dp)

    def w_send(j, role, src, dst, dp, dq):
        send(src, dst, w_s, w_r.at[j, ROUND[role]], w_dev(j, dp, dq))

    def w_arrived(j, n, pieces):
        arrived(wbuf.at[pl.ds(j * 16, pieces)], w_r.at[j, n])

    lower, upper = pl.ds(0, 32), pl.ds(32, 32)

    def stage1(j):
        p, q = coords(j)
        src, dst = w_source(j), piece(j, p, q)
        w_send(j, PA, src, dst, 1, 0)
        w_send(j, PB, src, dst, 3, 0)

    def stage1q(j):
        p, q = coords(j)
        src, dst = w_source(j), piece(j, p, q)
        w_send(j, QA, src, dst, 0, 1)
        w_send(j, QB, src, dst, 0, 3)

    def stage2(j):
        p, q = coords(j)
        a, b = piece(j, add(p, 3), q), piece(j, add(p, 1), q)
        w_arrived(j, 0, 2)
        w_send(j, PH0, a.at[lower], a.at[lower], 1, 0)
        w_send(j, PH1, b.at[upper], b.at[upper], 3, 0)
        w_send(j, QA + 1, a, a, 0, 1)
        w_send(j, QB + 1, a, a, 0, 3)
        w_send(j, QA + 2, b, b, 0, 1)
        w_send(j, QB + 2, b, b, 0, 3)

    def stage3(j):
        p, q = coords(j)
        a = piece(j, add(p, 2), q)
        w_arrived(j, 1, 1)
        w_send(j, QA + 3, a, a, 0, 1)
        w_send(j, QB + 3, a, a, 0, 3)

    order = (0, 3, 1, 2)

    def relay(j, i):
        p, q = coords(j)
        a = piece(j, add(p, order[i]), add(q, 3))
        b = piece(j, add(p, order[i]), add(q, 1))
        w_send(j, RA + i, a.at[lower], a.at[lower], 0, 1)
        w_send(j, RB + i, b.at[upper], b.at[upper], 0, 3)

    def stage4(j):
        w_arrived(j, 2, 6)
        for i in range(3):
            relay(j, i)

    def stage5(j):
        w_arrived(j, 3, 2)
        relay(j, 3)

    def stage6(j):
        w_arrived(j, 4, 4)
    stage1(0)
    stage1(1)
    load_emb.wait()

    def norm_rows(b, carry):
        rows = pl.ds(pl.multiple_of(b * 32, 32), 32)
        values = emb[rows, :].astype(F32)
        inv = lax.rsqrt(jnp.mean(values * values, axis=-1, keepdims=True) + 1e-06)
        normed[rows, :] = (values * inv * gain_ref[...]).astype(BF16)
        return carry
    lax.fori_loop(0, 4, norm_rows, 0)
    arrived(ids.at[chip, 1 - k], ir_sem)
    for d in chips:
        send(ids.at[chip], ids.at[chip], i_s, i_r, chip_dev(*d))
    stage1q(0)
    stage1q(1)
    lax.fori_loop(4, 16, norm_rows, 0)
    stage2(0)
    stage2(1)
    table = dot_t(sel[...], normed[...]).astype(BF16)
    tab[0 : 3 * CH, :] = table[:, 0:256]
    tab[3 * CH : 6 * CH, :] = table[:, 256:512]

    own_hot = lax.broadcasted_iota(jnp.int32, (VOCAB, 128), 0) == ids_ref[...]
    own_hot = jnp.where(own_hot, 1.0, 0.0).astype(F32).T.astype(BF16)
    resid[...] = jnp.dot(own_hot, emb[...], preferred_element_type=F32).astype(BF16)
    arrived(ids.at[pl.ds(0, 63)], i_r)

    lane = lax.broadcasted_iota(jnp.int32, (3 * CH, 128), 1).astype(F32).astype(BF16)
    not_first, not_two = lane >= 1, lane >= 2
    none = jnp.zeros((3 * CH, 128), BF16)
    vocab = lax.broadcasted_iota(jnp.int32, (256, 128), 0).astype(F32).astype(BF16)
    one, zero = jnp.ones((256, 128), BF16), jnp.zeros((256, 128), BF16)

    def mix_window(src_line, zz, h):
        hots, highs = [], []
        for b in range(4):
            row = ids[src_line * 4 + h * 2 + b // 2, b % 2]
            low = jnp.broadcast_to((row & 255).astype(F32).astype(BF16), (256, 128))
            hots.append(jnp.where(vocab == low, one, zero))
            highs.append(row >> 8)
        both = jnp.dot(tab[...], jnp.concatenate(hots, axis=1), preferred_element_type=F32)
        n = zz * 2 + h
        last1 = last2 = none
        for b in range(4):
            cols = slice(b * 128, (b + 1) * 128)
            now = jnp.where(highs[b] == 1, both[3 * CH :, cols], both[: 3 * CH, cols])
            packed = now.astype(BF16)
            roll1, roll2 = pltpu.roll(packed, 1, 1), pltpu.roll(packed, 2, 1)
            back1 = jnp.where(not_first, roll1, last1)
            back2 = jnp.where(not_two, roll2, last2)
            last1, last2 = roll1, roll2
            feat = tapb[0] * now + tapb[1] * back1.astype(F32) + tapb[2] * back2.astype(F32)
            pr = (feat[CH : 2 * CH] * feat[2 * CH :]).astype(BF16)
            for g in range(2):
                rows = slice(g * GROUP, (g + 1) * GROUP)
                qf[g, n, :, cols] = feat[rows]
                prod[g, n, :, cols] = pr[rows]

    def mix_rows(yy):
        def one_line(zz, carry):
            for h in range(2):
                mix_window(yy * 4 + zz, zz, h)
            return carry

        lax.fori_loop(0, 4, one_line, 0)
        for g in range(2):
            p = prod[g].reshape(128, LEN)
            first = jnp.dot(p[:, :256], toep[g, 128:], preferred_element_type=F32)
            second = jnp.dot(p[:, 128:], toep[g], preferred_element_type=F32)
            filt = jnp.concatenate([first, second], axis=1).reshape(8, GROUP, LEN)
            for n in range(8):
                gated = (qf[g, n] * filt[n]).astype(BF16)
                for b in range(4):
                    lanes = ((b % 2) * 4 + (n % 2) * 2 + b // 2) * 128
                    gsend[yy * 4 + n // 2, g * GROUP : (g + 1) * GROUP, lanes : lanes + 128] = (
                        gated[:, b * 128 : (b + 1) * 128]
                    )

    my_rows = pl.ds(pl.multiple_of(k * CH, CH), CH)
    sib_rows = pl.ds(pl.multiple_of((1 - k) * CH, CH), CH)

    half_lanes = (pl.ds(0, LEN), pl.ds(LEN, LEN))

    def scatter(dy, t):
        yy = add(y, dy)
        for dz in range(4):
            if (dy, dz) == (0, 0):
                continue
            send(gsend.at[yy * 4 + add(z, dz), :, half_lanes[t]],
                 gath.at[line, my_rows, half_lanes[t]],
                 g_s, g_r.at[t, dy], plane_dev(dy, dz))

    polls = {2: lambda: (stage3(0),stage3(1),),1: lambda: (stage4(0),stage4(1),),3: lambda: (None,),0: lambda: (stage5(0),stage5(1),)}
    for dy in (2, 1, 3, 0):
        mix_rows(add(y, dy))
        scatter(dy, 0)
        polls[dy]()

    own_g = pltpu.make_async_copy(gsend.at[line], gath.at[line, my_rows], gl_sem)
    own_g.start()

    def row_of(dy):
        return pl.ds(pl.multiple_of(add(y, 4 - dy) * 4, 4), 4)

    def hand_over(t):
        lanes = half_lanes[t]
        for dy in (2, 1, 3, 0):
            arrived(gath.at[pl.ds(0, 4 if dy else 3), my_rows, lanes], g_r.at[t, dy])
            if t == 0 and dy == 0:
                own_g.wait()
            there = gath.at[row_of(dy), my_rows, lanes]
            send(there, there, b_s, b_r.at[t, dy], line_dev(0, 1))

    def fill_lhs(t):
        lanes = half_lanes[t]
        for dy in (2, 1, 3, 0):
            sy = add(y, 4 - dy)
            arrived(gath.at[row_of(dy), sib_rows, lanes], b_r.at[t, dy])
            for pair in range(2):
                block = jnp.concatenate(
                    [gath[sy * 4 + 2 * pair, :, lanes], gath[sy * 4 + 2 * pair + 1, :, lanes]],
                    axis=0,
                )
                cols = pl.multiple_of(sy * 256 + pair * 128, 128)
                lhs[t * LEN : (t + 1) * LEN, pl.ds(cols, 128)] = block.T

    def w_ready(j):
        stage6(j)

    def multiply(t, j):

        def times(dx):
            w = wbuf[j * 16 : (j + 1) * 16].reshape(16 * 64, CW)
            rows = pl.ds(pl.multiple_of(t * LEN + add(x, dx) * 128, 128), 128)
            return jnp.dot(lhs[rows, :], w, preferred_element_type=F32)

        far = times(2).astype(BF16)
        for side, dx in ((0, 1), (1, 3)):
            opp_s[j, t, side] = far[:, side * 256 : (side + 1) * 256]
            send(opp_s.at[j, t, side], opp_r.at[j, t, side],
                 o_s, o_r.at[j, t], line_dev(dx, 0))
        part[j, t, 0] = times(1)
        part[j, t, 1] = times(3)
        mine[t, j, k] = times(0).astype(BF16)
        if t == 1:
            send(mine.at[1 - k, j, k], mine.at[1 - k, j, k], m_s, m_r.at[j], line_dev(0, 1))

    def pass_on(t, j):
        arrived(opp_r.at[j, t], o_r.at[j, t])
        for side, dx in ((0, 1), (1, 3)):
            half = slice(side * 256, (side + 1) * 256)
            rest = slice((1 - side) * 256, (2 - side) * 256)
            fin_s[j, t, side, :, rest] = part[j, t, side, :, rest].astype(BF16)
            fin_s[j, t, side, :, half] = (
                part[j, t, side, :, half] + opp_r[j, t, side].astype(F32)
            ).astype(BF16)
            send(fin_s.at[j, t, side], fin_r.at[j, side, k],
                 f_s, f_r.at[j], dev(add(x, dx), y, z, t))

    def finish(j):
        arrived(mine.at[k, j, 1 - k], m_r.at[j])
        arrived(fin_r.at[j], f_r.at[j])
        for h in range(2):
            cols = slice(h * CHUNKS * CW + j * CW, h * CHUNKS * CW + (j + 1) * CW)
            total = (
                fin_r[j, 0, h].astype(F32) + fin_r[j, 1, h].astype(F32)
                + mine[k, j, h].astype(F32) + resid[:, cols].astype(F32)
            )
            out_ref[:, cols] = total.astype(BF16)
    hand_over(0)
    for dy in (2, 1, 3, 0):
        scatter(dy, 1)
    stage1(2)
    stage1(3)
    fill_lhs(0)
    pltpu.make_async_copy(wbuf.at[pl.ds(0, CHUNKS)], wbuf.at[pl.ds(0, CHUNKS)], wl_sem).wait()
    w_ready(0)
    multiply(0, 0)
    w_ready(1)
    multiply(0, 1)
    pass_on(0, 0)
    stage1q(2)
    stage1q(3)
    pass_on(0, 1)
    hand_over(1)
    stage2(2)
    stage2(3)
    fill_lhs(1)
    multiply(1, 0)
    multiply(1, 1)
    stage3(2)
    stage3(3)
    pass_on(1, 0)
    stage4(2)
    stage4(3)
    pass_on(1, 1)
    stage5(2)
    stage5(3)
    w_ready(2)
    multiply(0, 2)
    multiply(1, 2)
    w_ready(3)
    multiply(0, 3)
    pass_on(0, 2)
    multiply(1, 3)
    pass_on(1, 2)
    pass_on(0, 3)
    pass_on(1, 3)
    for j in range(CHUNKS):
        finish(j)
    all_sent(ids.at[chip, k], is_sem)
    all_sent(ids.at[pl.ds(0, 63)], i_s)
    all_sent(wbuf.at[pl.ds(0, 15 * CHUNKS)], w_s)
    all_sent(gath.at[pl.ds(0, 15), pl.ds(0, CH), :], g_s)
    all_sent(gath.at[:, pl.ds(0, CH), :], b_s)
    all_sent(opp_s, o_s)
    all_sent(fin_s, f_s)
    all_sent(mine.at[0, :, 0], m_s)


def per_device(token_ids, embedding, norm_gain, in_proj, short_taps, conv_taps, out_proj):
    vmem = pl.BlockSpec(memory_space=pltpu.VMEM)
    hbm = pl.BlockSpec(memory_space=pltpu.HBM)
    dma = pltpu.SemaphoreType.DMA
    out = pl.pallas_call(
        kernel,
        out_shape=jax.ShapeDtypeStruct((128, D), BF16),
        in_specs=[hbm] * 7,
        out_specs=vmem,
        scratch_shapes=[
            pltpu.VMEM((1, 128), jnp.int32),
            pltpu.VMEM((1, D), F32),
            pltpu.VMEM((SHORT, 3, 128), F32),
            pltpu.VMEM((8, 128), BF16),
            pltpu.VMEM((VOCAB, D), BF16),
            pltpu.VMEM((3, D, 128), BF16),
            pltpu.VMEM((VOCAB, D), BF16),
            pltpu.VMEM((3 * CH, D), BF16),
            pltpu.VMEM((6 * CH, 256), BF16),
            pltpu.VMEM((64, 2, 1, 128), jnp.int32),
            pltpu.VMEM((128, 128), F32),
            pltpu.VMEM((SHORT, 3 * CH, 128), F32),
            pltpu.VMEM((2, 384, 256), BF16),
            pltpu.VMEM((2, 8, GROUP, LEN), BF16),
            pltpu.VMEM((2, 8, GROUP, LEN), F32),
            pltpu.VMEM((16, CH, 2 * LEN), BF16),
            pltpu.VMEM((16, 2 * CH, 2 * LEN), BF16),
            pltpu.VMEM((2 * LEN, 1024), BF16),
            pltpu.VMEM((CHUNKS * 16, 64, CW), BF16),
            pltpu.VMEM((CHUNKS, 2, 2, 128, 256), BF16),
            pltpu.VMEM((CHUNKS, 2, 2, 128, 256), BF16),
            pltpu.VMEM((CHUNKS, 2, 2, 128, CW), F32),
            pltpu.VMEM((CHUNKS, 2, 2, 128, CW), BF16),
            pltpu.VMEM((CHUNKS, 2, 2, 128, CW), BF16),
            pltpu.VMEM((2, CHUNKS, 2, 128, CW), BF16),
            pltpu.VMEM((128, D), BF16),
            dma((7,)), dma((N_ONE,)), dma((CHUNKS, 5)), dma((2, 4)), dma((2, 4)),
            dma((CHUNKS, 2)), dma((CHUNKS,)), dma((CHUNKS,)),
        ],
        compiler_params=pltpu.CompilerParams(
            collective_id=0, has_side_effects=True, vmem_limit_bytes=46 * 1024 * 1024
        ),
        name="mixer",
    )(*(
        pltpu.with_memory_space_constraint(v, pltpu.HBM)
        for v in (token_ids, norm_gain.reshape(1, D), short_taps, conv_taps, embedding,
                  in_proj, out_proj)
    ))
    return out[None]


def solution(mesh):
    return jax.shard_map(
        per_device,
        mesh=mesh,
        in_specs=(
            P("fsdp", "ctx"),
            P(),
            P(),
            P(None, None, "fsdp"),
            P(None, None, "fsdp"),
            P("fsdp", None),
            P("fsdp", None),
        ),
        out_specs=P("fsdp", "ctx", None),
        check_vma=False,
    )
```

```python
import jax
import jax.numpy as jnp
from jax import lax
from jax.experimental import pallas as pl
from jax.experimental.pallas import tpu as pltpu
from jax.sharding import PartitionSpec as P

GROUP = 16
TAPS = 128
SHORT = 3
VOCAB = 512
D = 4096
LEN = 512
CH = 32
CHUNKS = 4
CW = 512
F32 = jnp.float32
BF16 = jnp.bfloat16
MESH = pl.DeviceIdType.MESH

PA, PB, PH0, PH1, QA, QB, RA, RB = 0, 1, 2, 3, 4, 8, 12, 16
ROUND = {PA: 0, PB: 0, PH0: 1, PH1: 1, QA: 2, QA + 1: 2, QA + 2: 2, QA + 3: 3,
         QB: 2, QB + 1: 2, QB + 2: 2, QB + 3: 3, **{RA + i: 4 for i in range(8)}}
N_ONE = 12


def dot_t(a, b):
    return lax.dot_general(a, b, (((1,), (1,)), ((), ())), preferred_element_type=F32)


def kernel(
    ids_in, gain_in, staps_in, ctaps_in, emb_ref, inp_ref, op_ref, out_ref,
    ids_ref, gain_ref, staps_ref, ctaps_ref,
    emb, inp, normed, sel, tab, ids, taps, tapb, toep, prod, qf, gsend, gath, lhs, wbuf,
    opp_s, opp_r, part, fin_s, fin_r, mine, resid,
    ld_sem, one_sem, w_r, g_r, b_r, o_r, f_r, m_r,
):
    wl_sem, gl_sem, is_sem, ir_sem, i_s, i_r, w_s, g_s, b_s, o_s, f_s, m_s = (
        one_sem.at[i] for i in range(N_ONE)
    )
    f = lax.axis_index("fsdp")
    c = lax.axis_index("ctx")
    xh, y, z = f // 16, (f // 4) % 4, f % 4
    xl, k = c // 2, c % 2
    x = xh * 2 + xl
    line = y * 4 + z

    def dev(xx, yy, zz, kk):
        return {"fsdp": (xx // 2) * 16 + yy * 4 + zz, "ctx": (xx % 2) * 2 + kk}

    def add(a, n):
        return (a + n) % 4

    def remote(src, dst, ssem, rsem, target):
        return pltpu.make_async_remote_copy(
            src_ref=src, dst_ref=dst, send_sem=ssem, recv_sem=rsem,
            device_id=target, device_id_type=MESH,
        )

    here = {"fsdp": f, "ctx": c}
    def send(src, dst, ssem, rsem, target):
        remote(src, dst, ssem, rsem, target).start()

    def arrived(dst, rsem):
        remote(dst, dst, rsem, rsem, here).wait_recv()

    def all_sent(src, ssem):
        remote(src, src, ssem, ssem, here).wait_send()

    def line_dev(dx, dk):
        return dev(add(x, dx), y, z, (k + dk) % 2)

    def plane_dev(dy, dz):
        return dev(x, add(y, dy), add(z, dz), k)

    chip = line * 4 + x

    small = []
    for i, (src, dst) in enumerate((
        (ids_in, ids_ref), (staps_in, staps_ref), (ctaps_in, ctaps_ref), (gain_in, gain_ref)
    )):
        small.append(pltpu.make_async_copy(src, dst, ld_sem.at[2 + i]))
        small[-1].start()
    load_inp = pltpu.make_async_copy(inp_ref, inp, ld_sem.at[0])
    load_inp.start()
    load_emb = pltpu.make_async_copy(emb_ref, emb, ld_sem.at[1])
    load_emb.start()

    def w_source(j):
        cols = pl.multiple_of(k * (CHUNKS * CW) + j * CW, CW)
        return op_ref.at[pl.ds(pl.multiple_of(xl * 64, 64), 64), pl.ds(cols, CW)]

    for j in range(CHUNKS):
        pltpu.make_async_copy(w_source(j), wbuf.at[j * 16 + line], wl_sem).start()
    own_ids = pltpu.make_async_copy(ids_in, ids.at[chip, k], ld_sem.at[6])
    own_ids.start()

    xs = [add(x, i) for i in range(4)]
    ctxs = [(xx % 2) * 2 + k for xx in xs]
    fsdps = [(xx // 2) * 16 for xx in xs]
    rows = [add(y, i) * 4 for i in range(4)]
    cols = [add(z, i) for i in range(4)]
    chips = [(dx, dy, dz) for dy in range(4) for dz in range(4) for dx in range(4)][1:]

    def chip_dev(dx, dy, dz):
        return {"fsdp": fsdps[dx] + rows[dy] + cols[dz], "ctx": ctxs[dx]}

    barrier = pltpu.get_barrier_semaphore()
    for dx in (0, 1, 3):
        pl.semaphore_signal(barrier, inc=1, device_id=line_dev(dx, 1), device_id_type=MESH)
    for d in chips:
        pl.semaphore_signal(barrier, inc=1, device_id=chip_dev(*d), device_id_type=MESH)
    for copy in small:
        copy.wait()
    staps = jnp.concatenate(
        [staps_ref[j, :, :] for j in range(SHORT)] + [jnp.zeros((128 - 9, 128), F32)], axis=0
    )
    taps[...] = staps.T
    ch0 = pl.multiple_of(c * CH, CH)
    my_taps = taps[pl.ds(ch0, CH), :]
    for j in range(SHORT):
        for i in range(3):
            tapb[j, i * CH : (i + 1) * CH, :] = jnp.broadcast_to(
                my_taps[:, 3 * j + i : 3 * j + i + 1], (CH, 128)
            )

    all_taps = ctaps_ref[...].astype(F32)
    rows8 = lax.broadcasted_iota(jnp.int32, (8, 128), 0)
    for g in range(2):
        row = jnp.sum(jnp.where(rows8 == 2 * c + g, all_taps, 0.0), axis=0, keepdims=True)
        base = jnp.concatenate([row, jnp.zeros((1, 384), F32)], axis=1)
        base = jnp.broadcast_to(base, (384, 512))
        band = pltpu.roll(base, 384, 1, stride=1, stride_axis=0)
        toep[g] = band[:, :256].astype(BF16)

    load_inp.wait()
    pick = (
        lax.broadcasted_iota(jnp.int32, (CH, 128), 1)
        == lax.broadcasted_iota(jnp.int32, (CH, 128), 0) + ch0
    )
    pick = jnp.where(pick, 1.0, 0.0).astype(BF16)
    for i in range(3):
        for d0 in range(0, D, 1024):
            sel[i * CH : (i + 1) * CH, d0 : d0 + 1024] = dot_t(
                pick, inp[i, d0 : d0 + 1024, :]
            ).astype(BF16)
    pl.semaphore_wait(barrier, 66)
    own_ids.wait()
    send(ids_ref, ids.at[chip, k], is_sem, ir_sem, line_dev(0, 1))

    def piece(j, p, q):
        return wbuf.at[j * 16 + (p * 4 + q if j % 2 == 0 else q * 4 + p)]

    def coords(j):
        return (y, z) if j % 2 == 0 else (z, y)

    def w_dev(j, dp, dq):
        return plane_dev(dp, dq) if j % 2 == 0 else plane_dev(dq, dp)

    def w_send(j, role, src, dst, dp, dq):
        send(src, dst, w_s, w_r.at[j, ROUND[role]], w_dev(j, dp, dq))

    def w_arrived(j, n, pieces):
        arrived(wbuf.at[pl.ds(j * 16, pieces)], w_r.at[j, n])

    lower, upper = pl.ds(0, 32), pl.ds(32, 32)

    def stage1(j):
        p, q = coords(j)
        src, dst = w_source(j), piece(j, p, q)
        w_send(j, PA, src, dst, 1, 0)
        w_send(j, PB, src, dst, 3, 0)

    def stage1q(j):
        p, q = coords(j)
        src, dst = w_source(j), piece(j, p, q)
        w_send(j, QA, src, dst, 0, 1)
        w_send(j, QB, src, dst, 0, 3)

    def stage2(j):
        p, q = coords(j)
        a, b = piece(j, add(p, 3), q), piece(j, add(p, 1), q)
        w_arrived(j, 0, 2)
        w_send(j, PH0, a.at[lower], a.at[lower], 1, 0)
        w_send(j, PH1, b.at[upper], b.at[upper], 3, 0)
        w_send(j, QA + 1, a, a, 0, 1)
        w_send(j, QB + 1, a, a, 0, 3)
        w_send(j, QA + 2, b, b, 0, 1)
        w_send(j, QB + 2, b, b, 0, 3)

    def stage3(j):
        p, q = coords(j)
        a = piece(j, add(p, 2), q)
        w_arrived(j, 1, 1)
        w_send(j, QA + 3, a, a, 0, 1)
        w_send(j, QB + 3, a, a, 0, 3)

    order = (0, 3, 1, 2)

    def relay(j, i):
        p, q = coords(j)
        a = piece(j, add(p, order[i]), add(q, 3))
        b = piece(j, add(p, order[i]), add(q, 1))
        w_send(j, RA + i, a.at[lower], a.at[lower], 0, 1)
        w_send(j, RB + i, b.at[upper], b.at[upper], 0, 3)

    def stage4(j):
        w_arrived(j, 2, 6)
        for i in range(3):
            relay(j, i)

    def stage5(j):
        w_arrived(j, 3, 2)
        relay(j, 3)

    def stage6(j):
        w_arrived(j, 4, 4)
    stage1(0)
    stage1(1)
    load_emb.wait()

    def norm_rows(b, carry):
        rows = pl.ds(pl.multiple_of(b * 32, 32), 32)
        values = emb[rows, :].astype(F32)
        inv = lax.rsqrt(jnp.mean(values * values, axis=-1, keepdims=True) + 1e-06)
        normed[rows, :] = (values * inv * gain_ref[...]).astype(BF16)
        return carry
    lax.fori_loop(0, 4, norm_rows, 0)
    arrived(ids.at[chip, 1 - k], ir_sem)
    for d in chips:
        send(ids.at[chip], ids.at[chip], i_s, i_r, chip_dev(*d))
    stage1q(0)
    stage1q(1)
    lax.fori_loop(4, 16, norm_rows, 0)
    stage2(0)
    stage2(1)
    table = dot_t(sel[...], normed[...]).astype(BF16)
    tab[0 : 3 * CH, :] = table[:, 0:256]
    tab[3 * CH : 6 * CH, :] = table[:, 256:512]

    own_hot = lax.broadcasted_iota(jnp.int32, (VOCAB, 128), 0) == ids_ref[...]
    own_hot = jnp.where(own_hot, 1.0, 0.0).astype(F32).T.astype(BF16)
    resid[...] = jnp.dot(own_hot, emb[...], preferred_element_type=F32).astype(BF16)
    arrived(ids.at[pl.ds(0, 63)], i_r)

    lane = lax.broadcasted_iota(jnp.int32, (3 * CH, 128), 1).astype(F32).astype(BF16)
    not_first, not_two = lane >= 1, lane >= 2
    none = jnp.zeros((3 * CH, 128), BF16)
    vocab = lax.broadcasted_iota(jnp.int32, (256, 128), 0).astype(F32).astype(BF16)
    one, zero = jnp.ones((256, 128), BF16), jnp.zeros((256, 128), BF16)

    def mix_window(src_line, zz, h):
        hots, highs = [], []
        for b in range(4):
            row = ids[src_line * 4 + h * 2 + b // 2, b % 2]
            low = jnp.broadcast_to((row & 255).astype(F32).astype(BF16), (256, 128))
            hots.append(jnp.where(vocab == low, one, zero))
            highs.append(row >> 8)
        both = jnp.dot(tab[...], jnp.concatenate(hots, axis=1), preferred_element_type=F32)
        n = zz * 2 + h
        last1 = last2 = none
        for b in range(4):
            cols = slice(b * 128, (b + 1) * 128)
            now = jnp.where(highs[b] == 1, both[3 * CH :, cols], both[: 3 * CH, cols])
            packed = now.astype(BF16)
            roll1, roll2 = pltpu.roll(packed, 1, 1), pltpu.roll(packed, 2, 1)
            back1 = jnp.where(not_first, roll1, last1)
            back2 = jnp.where(not_two, roll2, last2)
            last1, last2 = roll1, roll2
            feat = tapb[0] * now + tapb[1] * back1.astype(F32) + tapb[2] * back2.astype(F32)
            pr = (feat[CH : 2 * CH] * feat[2 * CH :]).astype(BF16)
            for g in range(2):
                rows = slice(g * GROUP, (g + 1) * GROUP)
                qf[g, n, :, cols] = feat[rows]
                prod[g, n, :, cols] = pr[rows]

    def mix_rows(yy):
        def one_line(zz, carry):
            for h in range(2):
                mix_window(yy * 4 + zz, zz, h)
            return carry

        lax.fori_loop(0, 4, one_line, 0)
        for g in range(2):
            p = prod[g].reshape(128, LEN)
            first = jnp.dot(p[:, :256], toep[g, 128:], preferred_element_type=F32)
            second = jnp.dot(p[:, 128:], toep[g], preferred_element_type=F32)
            filt = jnp.concatenate([first, second], axis=1).reshape(8, GROUP, LEN)
            for n in range(8):
                gated = (qf[g, n] * filt[n]).astype(BF16)
                for b in range(4):
                    lanes = ((b % 2) * 4 + (n % 2) * 2 + b // 2) * 128
                    gsend[yy * 4 + n // 2, g * GROUP : (g + 1) * GROUP, lanes : lanes + 128] = (
                        gated[:, b * 128 : (b + 1) * 128]
                    )

    my_rows = pl.ds(pl.multiple_of(k * CH, CH), CH)
    sib_rows = pl.ds(pl.multiple_of((1 - k) * CH, CH), CH)

    half_lanes = (pl.ds(0, LEN), pl.ds(LEN, LEN))

    def scatter(dy, t):
        yy = add(y, dy)
        for dz in range(4):
            if (dy, dz) == (0, 0):
                continue
            send(gsend.at[yy * 4 + add(z, dz), :, half_lanes[t]],
                 gath.at[line, my_rows, half_lanes[t]],
                 g_s, g_r.at[t, dy], plane_dev(dy, dz))

    polls = {2: lambda: (stage3(0),stage3(1),),1: lambda: (stage4(0),stage4(1),),3: lambda: (None,),0: lambda: (stage5(0),stage5(1),)}
    for dy in (2, 1, 3, 0):
        mix_rows(add(y, dy))
        scatter(dy, 0)
        polls[dy]()

    own_g = pltpu.make_async_copy(gsend.at[line], gath.at[line, my_rows], gl_sem)
    own_g.start()

    def row_of(dy):
        return pl.ds(pl.multiple_of(add(y, 4 - dy) * 4, 4), 4)

    def hand_over(t):
        lanes = half_lanes[t]
        for dy in (2, 1, 3, 0):
            arrived(gath.at[pl.ds(0, 4 if dy else 3), my_rows, lanes], g_r.at[t, dy])
            if t == 0 and dy == 0:
                own_g.wait()
            there = gath.at[row_of(dy), my_rows, lanes]
            send(there, there, b_s, b_r.at[t, dy], line_dev(0, 1))

    def fill_lhs(t):
        lanes = half_lanes[t]
        for dy in (2, 1, 3, 0):
            sy = add(y, 4 - dy)
            arrived(gath.at[row_of(dy), sib_rows, lanes], b_r.at[t, dy])
            for pair in range(2):
                block = jnp.concatenate(
                    [gath[sy * 4 + 2 * pair, :, lanes], gath[sy * 4 + 2 * pair + 1, :, lanes]],
                    axis=0,
                )
                cols = pl.multiple_of(sy * 256 + pair * 128, 128)
                lhs[t * LEN : (t + 1) * LEN, pl.ds(cols, 128)] = block.T

    def w_ready(j):
        stage6(j)

    def multiply(t, j):

        def times(dx):
            w = wbuf[j * 16 : (j + 1) * 16].reshape(16 * 64, CW)
            rows = pl.ds(pl.multiple_of(t * LEN + add(x, dx) * 128, 128), 128)
            return jnp.dot(lhs[rows, :], w, preferred_element_type=F32)

        far = times(2).astype(BF16)
        for side, dx in ((0, 1), (1, 3)):
            opp_s[j, t, side] = far[:, side * 256 : (side + 1) * 256]
            send(opp_s.at[j, t, side], opp_r.at[j, t, side],
                 o_s, o_r.at[j, t], line_dev(dx, 0))
        part[j, t, 0] = times(1)
        part[j, t, 1] = times(3)
        mine[t, j, k] = times(0).astype(BF16)
        if t == 1:
            send(mine.at[1 - k, j, k], mine.at[1 - k, j, k], m_s, m_r.at[j], line_dev(0, 1))

    def pass_on(t, j):
        arrived(opp_r.at[j, t], o_r.at[j, t])
        for side, dx in ((0, 1), (1, 3)):
            half = slice(side * 256, (side + 1) * 256)
            rest = slice((1 - side) * 256, (2 - side) * 256)
            fin_s[j, t, side, :, rest] = part[j, t, side, :, rest].astype(BF16)
            fin_s[j, t, side, :, half] = (
                part[j, t, side, :, half] + opp_r[j, t, side].astype(F32)
            ).astype(BF16)
            send(fin_s.at[j, t, side], fin_r.at[j, side, k],
                 f_s, f_r.at[j], dev(add(x, dx), y, z, t))

    def finish(j):
        arrived(mine.at[k, j, 1 - k], m_r.at[j])
        arrived(fin_r.at[j], f_r.at[j])
        for h in range(2):
            cols = slice(h * CHUNKS * CW + j * CW, h * CHUNKS * CW + (j + 1) * CW)
            total = (
                fin_r[j, 0, h].astype(F32) + fin_r[j, 1, h].astype(F32)
                + mine[k, j, h].astype(F32) + resid[:, cols].astype(F32)
            )
            out_ref[:, cols] = total.astype(BF16)
    hand_over(0)
    for dy in (2, 1, 3, 0):
        scatter(dy, 1)
    stage1(2)
    stage1(3)
    fill_lhs(0)
    pltpu.make_async_copy(wbuf.at[pl.ds(0, CHUNKS)], wbuf.at[pl.ds(0, CHUNKS)], wl_sem).wait()
    w_ready(0)
    multiply(0, 0)
    w_ready(1)
    multiply(0, 1)
    pass_on(0, 0)
    stage1q(2)
    stage1q(3)
    pass_on(0, 1)
    hand_over(1)
    stage2(2)
    stage2(3)
    fill_lhs(1)
    multiply(1, 0)
    multiply(1, 1)
    stage3(2)
    stage3(3)
    pass_on(1, 0)
    stage4(2)
    stage4(3)
    pass_on(1, 1)
    stage5(2)
    stage5(3)
    w_ready(2)
    multiply(0, 2)
    multiply(1, 2)
    w_ready(3)
    multiply(0, 3)
    pass_on(0, 2)
    multiply(1, 3)
    pass_on(1, 2)
    pass_on(0, 3)
    finish(0)
    finish(1)
    pass_on(1, 3)
    finish(2)
    finish(3)
    all_sent(ids.at[chip, k], is_sem)
    all_sent(ids.at[pl.ds(0, 63)], i_s)
    all_sent(wbuf.at[pl.ds(0, 15 * CHUNKS)], w_s)
    all_sent(gath.at[pl.ds(0, 15), pl.ds(0, CH), :], g_s)
    all_sent(gath.at[:, pl.ds(0, CH), :], b_s)
    all_sent(opp_s, o_s)
    all_sent(fin_s, f_s)
    all_sent(mine.at[0, :, 0], m_s)


def per_device(token_ids, embedding, norm_gain, in_proj, short_taps, conv_taps, out_proj):
    vmem = pl.BlockSpec(memory_space=pltpu.VMEM)
    hbm = pl.BlockSpec(memory_space=pltpu.HBM)
    dma = pltpu.SemaphoreType.DMA
    out = pl.pallas_call(
        kernel,
        out_shape=jax.ShapeDtypeStruct((128, D), BF16),
        in_specs=[hbm] * 7,
        out_specs=vmem,
        scratch_shapes=[
            pltpu.VMEM((1, 128), jnp.int32),
            pltpu.VMEM((1, D), F32),
            pltpu.VMEM((SHORT, 3, 128), F32),
            pltpu.VMEM((8, 128), BF16),
            pltpu.VMEM((VOCAB, D), BF16),
            pltpu.VMEM((3, D, 128), BF16),
            pltpu.VMEM((VOCAB, D), BF16),
            pltpu.VMEM((3 * CH, D), BF16),
            pltpu.VMEM((6 * CH, 256), BF16),
            pltpu.VMEM((64, 2, 1, 128), jnp.int32),
            pltpu.VMEM((128, 128), F32),
            pltpu.VMEM((SHORT, 3 * CH, 128), F32),
            pltpu.VMEM((2, 384, 256), BF16),
            pltpu.VMEM((2, 8, GROUP, LEN), BF16),
            pltpu.VMEM((2, 8, GROUP, LEN), F32),
            pltpu.VMEM((16, CH, 2 * LEN), BF16),
            pltpu.VMEM((16, 2 * CH, 2 * LEN), BF16),
            pltpu.VMEM((2 * LEN, 1024), BF16),
            pltpu.VMEM((CHUNKS * 16, 64, CW), BF16),
            pltpu.VMEM((CHUNKS, 2, 2, 128, 256), BF16),
            pltpu.VMEM((CHUNKS, 2, 2, 128, 256), BF16),
            pltpu.VMEM((CHUNKS, 2, 2, 128, CW), F32),
            pltpu.VMEM((CHUNKS, 2, 2, 128, CW), BF16),
            pltpu.VMEM((CHUNKS, 2, 2, 128, CW), BF16),
            pltpu.VMEM((2, CHUNKS, 2, 128, CW), BF16),
            pltpu.VMEM((128, D), BF16),
            dma((7,)), dma((N_ONE,)), dma((CHUNKS, 5)), dma((2, 4)), dma((2, 4)),
            dma((CHUNKS, 2)), dma((CHUNKS,)), dma((CHUNKS,)),
        ],
        compiler_params=pltpu.CompilerParams(
            collective_id=0, has_side_effects=True, vmem_limit_bytes=46 * 1024 * 1024
        ),
        name="mixer",
    )(*(
        pltpu.with_memory_space_constraint(v, pltpu.HBM)
        for v in (token_ids, norm_gain.reshape(1, D), short_taps, conv_taps, embedding,
                  in_proj, out_proj)
    ))
    return out[None]


def solution(mesh):
    return jax.shard_map(
        per_device,
        mesh=mesh,
        in_specs=(
            P("fsdp", "ctx"),
            P(),
            P(),
            P(None, None, "fsdp"),
            P(None, None, "fsdp"),
            P("fsdp", None),
            P("fsdp", None),
        ),
        out_specs=P("fsdp", "ctx", None),
        check_vma=False,
    )
```
